256 devices in a mesh: kpt: 32 (over x, y, z_lo), aux: 8 (over z_hi, core).
Axes of the slice: x: 4, y: 4, z: 8 (z_hi: 4, z_lo: 2; z = z_hi * 2 + z_lo), core: 2. Of those that a mesh axis runs over, the one named last changes fastest.
Arguments:
- pair_tensors: bfloat16 [2, 64, 16, 512, 1024], P(None, 'kpt', 'aux'), may hold values from -0.1875 to 0.1875
- orbitals: bfloat16 [64, 512, 512], P('kpt'), may hold values from -6 to 6
- matchings: int32 [2, 64], replicated, may hold values from 0 to 63, as said below
Outputs:
- exchange: float32 [64, 2, 512, 512], P('kpt', None, 'aux')
The draws below stay inside these ranges and needn't reach their ends.
Inputs may be any that keep to these rules, and one draw needn't show every extreme that they name: Each row matchings[r] is a permutation of the 64 k-points. With 2^m = 32 blocks of 2 consecutive k-points, round r matches every k-point of block d with a k-point of block d XOR 2^(m - 1 - r).
All inputs are finite; a program needn't handle non-finite values.
Results may differ from the reference program's by a relative error of at most 0.00098.
Values may be sent and summed in bfloat16 or wider, within the bound.
A program may use at most 192 MiB of HBM per device.

```python
import jax
import jax.numpy as jnp
from jax import lax

NAO = 512
NOCC = 256
KPT_DEV = 2
ROUNDS = 2
KPTS = 64
NAUX = 16


def draw_matchings(key, part):
    blocks_count = KPTS // KPT_DEV
    bit_count = blocks_count.bit_length() - 1
    scores = jax.random.randint(key, (ROUNDS, blocks_count, KPT_DEV), 0, 2 ** 20, dtype=jnp.int32)
    scores = scores * KPT_DEV + jnp.arange(KPT_DEV, dtype=jnp.int32)
    within = jnp.argsort(scores, axis=-1, stable=True).astype(jnp.int32)
    block_ids = jnp.arange(blocks_count, dtype=jnp.int32)
    rows_out = []
    for which_round in range(ROUNDS):
        partner_block = jnp.bitwise_xor(block_ids, 1 << bit_count - 1 - which_round)
        matched = partner_block[:, None] * KPT_DEV + within[which_round]
        rows_out.append(matched.reshape(-1))
    return jnp.stack(rows_out, axis=0).astype(jnp.int32)


def level_of(rng, shape, cuts, smallest, largest):
    gain, own = 1.0, jax.random.fold_in(rng, 6)
    for axis_at, shards_of in cuts:
        draws = jnp.exp(jax.random.uniform(jax.random.fold_in(own, axis_at), (shards_of,), jnp.float32, smallest / len(cuts), largest / len(cuts)))
        gain = gain * jnp.repeat(draws, shape[axis_at] // shards_of).reshape([-1 if axis == axis_at else 1 for axis in range(len(shape))])
    return gain


def normal_values(own_key, shape, deviation, most, cuts=(), held_as=jnp.bfloat16):
    result = deviation * jax.random.normal(own_key, shape, jnp.float32)
    if cuts:
        result = result * level_of(own_key, shape, cuts, -0.22, 0.18)
    return jnp.clip(result, -most, most).astype(held_as)


def setup_inputs(seed: int = 0) -> dict:
    seeds = jax.random.split(jax.random.key(seed), 4)
    return {
        "pair_tensors": normal_values(seeds[0], (ROUNDS, KPTS, NAUX, NAO, 2 * NAO), (2 * NAO) ** -0.5, 0.1875, ((1, 32), (2, 8))),
        "orbitals": normal_values(seeds[1], (KPTS, NAO, 2 * NOCC), 1.0, 6.0, ((0, 32),)),
        "matchings": draw_matchings(jax.random.fold_in(seeds[3], 71), 0),
    }


def build_block(chosen):
    occupied = chosen.shape[-1] // 2
    real_part = chosen[..., :occupied]
    imag_part = chosen[..., occupied:]
    upper_rows = jnp.concatenate([real_part, imag_part], axis=-1)
    bottom = jnp.concatenate([-imag_part, real_part], axis=-1)
    return jnp.concatenate([upper_rows, bottom], axis=-2)


def reference(pair_tensors, orbitals, matchings):
    factor = 1.0 / (ROUNDS * NAUX * NOCC) ** 0.5
    high = lax.Precision.HIGHEST

    def one_point(index):
        running = jnp.zeros((2, NAO, NAO), jnp.float32)
        for which_round in range(ROUNDS):
            partner_id = matchings[which_round, index]
            chosen = lax.dynamic_index_in_dim(orbitals, partner_id, 0, keepdims=False)
            block = build_block(chosen).astype(jnp.float32)
            pairs = pair_tensors[which_round, index].astype(jnp.float32)
            half_done = jnp.einsum("pab,bc->pac", pairs, block, precision=high).astype(jnp.bfloat16)
            wide_half = half_done.astype(jnp.float32)
            real_half = wide_half[..., :NOCC]
            imag_half = wide_half[..., NOCC:]
            rotated = jnp.concatenate([-imag_half, real_half], axis=-1)
            exch_real = jnp.einsum("pac,pbc->ab", wide_half, wide_half, precision=high)
            exch_imag = jnp.einsum("pac,pbc->ab", wide_half, rotated, precision=high)
            running = running + jnp.stack([exch_real, exch_imag], axis=0) * factor
        return running

    return lax.map(one_point, jnp.arange(KPTS, dtype=jnp.int32))
```

```python
import functools

import jax
import jax.numpy as jnp
from jax import lax
from jax.experimental import pallas as pl
from jax.experimental.pallas import tpu as pltpu
from jax.sharding import PartitionSpec as P

MESH = pl.DeviceIdType.MESH
ROUNDS = 2
LEVELS = 32000.0
SMALLEST = 1e-30
PIECES = 4


def kernel(
    factor, pairs, orbs, match, out,
    held_pairs, c00, c01, c10, c11, block, halves, squares, scale_rows, scale_cols,
    codes, codes_in, scales, scales_in, total, handed,
    pair_sem, pair_send, pair_recv, x_send, x_recv, relay_send, relay_recv,
    share_send, share_recv, code_send, code_recv, scale_send, scale_recv, hand_send, hand_recv,
):
    kpt, aux = lax.axis_index("kpt"), lax.axis_index("aux")
    chip, core = aux // 2, aux % 2
    x = kpt // 8
    rest = kpt - x * 8
    near = (x + 1 - 2 * (x % 2)) * 8 + rest
    cross = (3 - x) * 8 + rest
    sibling = aux + 1 - 2 * core
    here = (kpt, sibling)
    nao, nocc = orbs.shape[1], orbs.shape[2] // 2
    width = nocc // 2
    rows = nao // PIECES
    naux = pairs.shape[2]
    combos = 2 * naux
    chosen = ((c00, c01), (c10, c11))

    def remote(src, dst, send, recv, device):
        return pltpu.make_async_remote_copy(
            src_ref=src, dst_ref=dst, send_sem=send, recv_sem=recv, device_id=device, device_id_type=MESH
        )

    def own_pair(r, p):
        return pltpu.make_async_copy(
            pairs.at[r, core, p], held_pairs.at[r, core * naux + p], pair_sem.at[r, p]
        )

    def given_pair(r, p):
        return remote(
            pairs.at[r, 1 - core, p], held_pairs.at[r, core * naux + p],
            pair_send.at[r, p], pair_recv.at[r, p], here,
        )

    def x_piece(q, t, part):
        return remote(
            orbs.at[core, pl.ds(t * rows, rows), pl.ds(part * nocc + q * width, width)],
            chosen[1][q].at[core, pl.ds(t * rows, rows), pl.ds(part * width, width)],
            x_send.at[q, t, part], x_recv.at[q, t, part], (near, aux),
        )

    def relay(q, t):
        return remote(
            chosen[1][q].at[core, pl.ds(t * rows, rows)], chosen[0][q].at[core, pl.ds(t * rows, rows)],
            relay_send.at[q, t], relay_recv.at[q, t], (cross, aux),
        )

    def share(r, q):
        return remote(
            chosen[r][q].at[core], chosen[r][q].at[core], share_send.at[r, q], share_recv.at[r, q], here
        )

    for r in (1, 0):
        for p in range(naux):
            own_pair(r, p).start()

    barrier = pltpu.get_barrier_semaphore()
    peers = [(kpt, lax.rem(chip + d, 4) * 2 + core) for d in (1, 2, 3)]
    for device in [(near, aux), (cross, aux), here] + peers:
        pl.semaphore_signal(barrier, inc=1, device_id=device, device_id_type=MESH)
    pl.semaphore_wait(barrier, 6)

    for q in range(2):
        for t in range(PIECES):
            for part in range(2):
                x_piece(q, t, part).start()
    for r in (1, 0):
        for p in range(naux):
            given_pair(r, p).start()
    squares[...] = jnp.zeros_like(squares)

    def pass_on(q, t):
        for part in range(2):
            x_piece(q, t, part).wait_recv()
        relay(q, t).start()

    def build(r, q):
        index = jnp.bitwise_and(match[r, kpt * 2 + core], 1)
        both = chosen[r][q][index]
        block[0:nao, :] = both
        block[nao:, 0:width] = -both[:, width:]
        block[nao:, width:] = both[:, 0:width]

    def transform(r, q, first, last):
        def step(p, carry):
            done = jnp.dot(held_pairs[r, p], block[...], preferred_element_type=jnp.float32).astype(jnp.bfloat16)
            real, imag = done[:, 0:width], done[:, width:]
            at = pl.multiple_of((r * combos + p) * 2 * nocc + q * 2 * width, 2 * width)
            halves[0:nao, pl.ds(at, 2 * width)] = done
            halves[nao:, pl.ds(at, 2 * width)] = jnp.concatenate([-imag, real], axis=1)
            wide_real, wide_imag = real.astype(jnp.float32), imag.astype(jnp.float32)
            squares[...] += wide_real * wide_real + wide_imag * wide_imag
            return carry

        lax.fori_loop(first, last, step, 0)

    for t in range(PIECES):
        pass_on(0, t)
    share(1, 0).start()
    for p in range(naux):
        own_pair(1, p).wait()
    for p in range(naux):
        given_pair(1, p).wait_recv()
    share(1, 0).wait_recv()
    build(1, 0)
    transform(1, 0, 0, naux)
    pass_on(1, 0)
    transform(1, 0, naux, combos)
    for t in range(PIECES):
        relay(0, t).wait_recv()
    share(0, 0).start()
    pass_on(1, 1)
    for p in range(naux):
        own_pair(0, p).wait()
    for p in range(naux):
        given_pair(0, p).wait_recv()
    share(0, 0).wait_recv()
    build(0, 0)
    transform(0, 0, 0, naux)
    pass_on(1, 2)
    transform(0, 0, naux, combos)
    pass_on(1, 3)
    share(1, 1).start()
    share(1, 1).wait_recv()
    build(1, 1)
    transform(1, 1, 0, combos)
    for t in range(PIECES):
        relay(1, t).wait_recv()
    share(0, 1).start()
    share(0, 1).wait_recv()
    build(0, 1)
    transform(0, 1, 0, combos)

    length = jnp.sqrt(jnp.maximum(jnp.sum(squares[...], axis=1, keepdims=True), SMALLEST))
    spread = jnp.broadcast_to(length, (nao, 128))
    gain = LEVELS ** 0.5
    scale_cols[...] = gain / spread
    for j in range(4):
        turned = spread[j * 128 : (j + 1) * 128, :].T[0:8, :]
        scales[:, j * 128 : (j + 1) * 128] = turned
        scale_rows[:, j * 128 : (j + 1) * 128] = gain / turned

    def offset(step):
        return 2 - step + 3 * (step // 2)

    def peer(step):
        return (kpt, lax.rem(chip + offset(step), 4) * 2 + core)

    def send_codes(step, part):
        return remote(
            codes.at[step, part], codes_in.at[step, part],
            code_send.at[step, part], code_recv.at[step, part], peer(step),
        )

    def send_scales(step):
        return remote(scales, scales_in.at[step], scale_send.at[step], scale_recv.at[step], peer(step))

    for step in range(3):
        send_scales(step).start()

    def products(owner, part):
        mine = halves[pl.ds(pl.multiple_of(owner * 128, 128), 128), :]
        return lax.dot_general(
            halves[part * nao : (part + 1) * nao, :], mine, (((1,), (1,)), ((), ())),
            preferred_element_type=jnp.float32,
        )

    def term(step, carry):
        owner = lax.rem(chip + offset(step), 4)
        down = scale_cols[pl.ds(pl.multiple_of(owner * 128, 128), 128), :]
        for part in range(2):
            sums = products(owner, part)
            for j in range(4):
                cols = slice(j * 128, (j + 1) * 128)
                scaled = sums[cols, :].T * down * scale_rows[0:1, cols]
                codes[step, part, :, cols] = jnp.round(scaled).astype(jnp.int32).astype(jnp.int16)
            send_codes(step, part).start()
        return carry

    lax.fori_loop(0, 3, term, 0)
    for part in range(2):
        sums = products(chip, part)
        for j in range(4):
            cols = slice(j * 128, (j + 1) * 128)
            total[part, :, cols] = sums[cols, :].T * factor

    def hand():
        return remote(handed, out.at[core], hand_send, hand_recv, here)

    for step in range(3):
        send_scales(step).wait()
        across = scales_in[step] * (factor / LEVELS)
        mine = jnp.broadcast_to(scales_in[step, 0:1, pl.ds(pl.multiple_of(chip * 128, 128), 128)], (128, 128)).T
        for part in range(2):
            send_codes(step, part).wait()
            for j in range(4):
                cols = slice(j * 128, (j + 1) * 128)
                wide = codes_in[step, part, :, cols].astype(jnp.int32).astype(jnp.float32)
                total[part, :, cols] += wide * mine * across[0:1, cols]
    for part in range(2):
        handed[part] = total[part, pl.ds(pl.multiple_of((1 - core) * 64, 64), 64), :]
    hand().start()
    for part in range(2):
        out[core, part] = total[part, pl.ds(pl.multiple_of(core * 64, 64), 64), :]

    for q in range(2):
        for t in range(PIECES):
            for part in range(2):
                x_piece(q, t, part).wait_send()
            relay(q, t).wait_send()
        for r in range(2):
            share(r, q).wait_send()
    for r in range(2):
        for p in range(naux):
            given_pair(r, p).wait_send()
    hand().wait()


def body(pairs, orbs, match):
    rounds, per_device, naux, nao, _ = pairs.shape
    nocc = orbs.shape[2] // 2
    factor = 1.0 / (rounds * naux * lax.axis_size("aux") * nocc) ** 0.5
    dma = pltpu.SemaphoreType.DMA
    combos = 2 * naux
    orbital_chunk = pltpu.VMEM((per_device, nao, nocc), jnp.bfloat16)
    return pl.pallas_call(
        functools.partial(kernel, factor),
        out_shape=jax.ShapeDtypeStruct((per_device, 2, nao // 8, nao), jnp.float32),
        in_specs=[
            pl.BlockSpec(memory_space=pl.ANY),
            pl.BlockSpec(memory_space=pl.ANY),
            pl.BlockSpec(memory_space=pltpu.SMEM),
        ],
        out_specs=pl.BlockSpec(memory_space=pltpu.VMEM),
        scratch_shapes=[
            pltpu.VMEM((rounds, combos, nao, 2 * nao), jnp.bfloat16),
            orbital_chunk, orbital_chunk, orbital_chunk, orbital_chunk,
            pltpu.VMEM((2 * nao, nocc), jnp.bfloat16),
            pltpu.VMEM((2 * nao, rounds * combos * 2 * nocc), jnp.bfloat16),
            pltpu.VMEM((nao, 128), jnp.float32),
            pltpu.VMEM((8, nao), jnp.float32),
            pltpu.VMEM((nao, 128), jnp.float32),
            pltpu.VMEM((3, 2, 128, nao), jnp.int16),
            pltpu.VMEM((3, 2, 128, nao), jnp.int16),
            pltpu.VMEM((8, nao), jnp.float32),
            pltpu.VMEM((3, 8, nao), jnp.float32),
            pltpu.VMEM((2, 128, nao), jnp.float32),
            pltpu.VMEM((2, 64, nao), jnp.float32),
            dma((rounds, naux)), dma((rounds, naux)), dma((rounds, naux)),
            dma((2, PIECES, 2)), dma((2, PIECES, 2)), dma((2, PIECES)), dma((2, PIECES)),
            dma((2, 2)), dma((2, 2)), dma((3, 2)), dma((3, 2)), dma((3,)), dma((3,)), dma, dma,
        ],
        compiler_params=pltpu.CompilerParams(
            collective_id=0, has_side_effects=True, vmem_limit_bytes=56 << 20
        ),
    )(pairs, orbs, match)


def solution(mesh):
    placed = (P(None, "kpt", "aux", None, None), P("kpt", None, None), P())
    return jax.shard_map(
        body, mesh=mesh, in_specs=placed, out_specs=P("kpt", None, "aux", None), check_vma=False
    )
```

```python
import functools

import jax
import jax.numpy as jnp
from jax import lax
from jax.experimental import pallas as pl
from jax.experimental.pallas import tpu as pltpu
from jax.sharding import PartitionSpec as P

MESH = pl.DeviceIdType.MESH
ROUNDS = 2
LEVELS = 32000.0
SMALLEST = 1e-30
PIECES = 4


def kernel(
    factor, pairs, orbs, match, out,
    held_pairs, c00, c01, c10, c11, block, halves, squares, scale_cols,
    codes, codes_in, scales, scales_in, sums_scale, other_scale, turned, total, sums, sums_in, handed,
    pair_sem, pair_send, pair_recv, x_send, x_recv, relay_send, relay_recv,
    share_send, share_recv, code_send, code_recv, scale_send, scale_recv, share_scale_sem,
    sum_send, sum_recv, hand_send, hand_recv,
):
    kpt, aux = lax.axis_index("kpt"), lax.axis_index("aux")
    chip, core = aux // 2, aux % 2
    x = kpt // 8
    rest = kpt - x * 8
    near = (x + 1 - 2 * (x % 2)) * 8 + rest
    cross = (3 - x) * 8 + rest
    sibling = aux + 1 - 2 * core
    here = (kpt, sibling)
    nao, nocc = orbs.shape[1], orbs.shape[2] // 2
    width = nocc // 2
    rows = nao // PIECES
    naux = pairs.shape[2]
    tile = nao // 4
    combos = 2 * naux
    chosen = ((c00, c01), (c10, c11))

    def remote(src, dst, send, recv, device):
        return pltpu.make_async_remote_copy(
            src_ref=src, dst_ref=dst, send_sem=send, recv_sem=recv, device_id=device, device_id_type=MESH
        )

    def own_pair(r, p):
        return pltpu.make_async_copy(
            pairs.at[r, core, p], held_pairs.at[r, core * naux + p], pair_sem.at[r, p]
        )

    def given_pair(r, p):
        return remote(
            pairs.at[r, 1 - core, p], held_pairs.at[r, core * naux + p],
            pair_send.at[r, p], pair_recv.at[r, p], here,
        )

    def x_piece(q, t, part):
        return remote(
            orbs.at[core, pl.ds(t * rows, rows), pl.ds(part * nocc + q * width, width)],
            chosen[1][q].at[core, pl.ds(t * rows, rows), pl.ds(part * width, width)],
            x_send.at[q, t, part], x_recv.at[q, t, part], (near, aux),
        )

    def relay(q, t):
        return remote(
            chosen[1][q].at[core, pl.ds(t * rows, rows)], chosen[0][q].at[core, pl.ds(t * rows, rows)],
            relay_send.at[q, t], relay_recv.at[q, t], (cross, aux),
        )

    def share(r, q):
        return remote(
            chosen[r][q].at[core], chosen[r][q].at[core], share_send.at[r, q], share_recv.at[r, q], here
        )

    for r in (1, 0):
        for p in range(naux):
            own_pair(r, p).start()

    barrier = pltpu.get_barrier_semaphore()
    peers = [(kpt, lax.rem(chip + d, 4) * 2 + side) for d in (1, 2, 3) for side in range(2)]
    for device in [(near, aux), (cross, aux), here] + peers:
        pl.semaphore_signal(barrier, inc=1, device_id=device, device_id_type=MESH)
    pl.semaphore_wait(barrier, 9)

    for q in range(2):
        for t in range(PIECES):
            for part in range(2):
                x_piece(q, t, part).start()
    for r in (1, 0):
        for p in range(naux):
            given_pair(r, p).start()
    squares[...] = jnp.zeros_like(squares)

    def pass_on(q, t):
        for part in range(2):
            x_piece(q, t, part).wait_recv()
        relay(q, t).start()

    def build(r, q):
        index = jnp.bitwise_and(match[r, kpt * 2 + core], 1)
        both = chosen[r][q][index]
        block[0:nao, :] = both
        block[nao:, 0:width] = -both[:, width:]
        block[nao:, width:] = both[:, 0:width]

    def transform(r, q, first, last):
        def step(p, carry):
            done = jnp.dot(held_pairs[r, p], block[...], preferred_element_type=jnp.float32).astype(jnp.bfloat16)
            real, imag = done[:, 0:width], done[:, width:]
            at = pl.multiple_of((r * combos + p) * 2 * nocc + q * 2 * width, 2 * width)
            halves[0:nao, pl.ds(at, 2 * width)] = done
            halves[nao:, pl.ds(at, 2 * width)] = jnp.concatenate([-imag, real], axis=1)
            wide_real, wide_imag = real.astype(jnp.float32), imag.astype(jnp.float32)
            squares[...] += wide_real * wide_real + wide_imag * wide_imag
            return carry

        lax.fori_loop(first, last, step, 0)

    for t in range(PIECES):
        pass_on(0, t)
    share(1, 0).start()
    for p in range(naux):
        own_pair(1, p).wait()
    for p in range(naux):
        given_pair(1, p).wait_recv()
    share(1, 0).wait_recv()
    build(1, 0)
    transform(1, 0, 0, naux)
    pass_on(1, 0)
    transform(1, 0, naux, combos)
    for t in range(PIECES):
        relay(0, t).wait_recv()
    share(0, 0).start()
    pass_on(1, 1)
    for p in range(naux):
        own_pair(0, p).wait()
    for p in range(naux):
        given_pair(0, p).wait_recv()
    share(0, 0).wait_recv()
    build(0, 0)
    transform(0, 0, 0, naux)
    pass_on(1, 2)
    transform(0, 0, naux, combos)
    pass_on(1, 3)
    share(1, 1).start()
    share(1, 1).wait_recv()
    build(1, 1)
    transform(1, 1, 0, combos)
    for t in range(PIECES):
        relay(1, t).wait_recv()
    share(0, 1).start()
    share(0, 1).wait_recv()
    build(0, 1)
    transform(0, 1, 0, combos)

    gain = LEVELS ** 0.5
    length = jnp.sqrt(jnp.maximum(jnp.sum(squares[...], axis=1, keepdims=True), SMALLEST))
    spread = jnp.broadcast_to(length, (nao, tile))
    scale_cols[...] = gain / spread
    for j in range(4):
        scales[:, j * tile : (j + 1) * tile] = spread[j * tile : (j + 1) * tile, :].T[0:8, :]

    def place(j):
        return pl.ds(pl.multiple_of(lax.rem(j, 4) * tile, tile), tile)

    def offset(step):
        return 2 - step + 3 * (step // 2)

    def peer(step):
        return (kpt, lax.rem(chip + offset(step), 4) * 2 + core)

    def send_scales(step):
        return remote(scales, scales_in.at[step], scale_send.at[step], scale_recv.at[step], peer(step))

    def share_scales():
        return remote(sums_scale, other_scale, share_scale_sem.at[0], share_scale_sem.at[1], here)

    for step in range(3):
        send_scales(step).start()

    def sources(owner):
        return (
            (lax.rem(owner + 1, 4), 0), (lax.rem(owner + 3, 4), 1), (lax.rem(owner + 2, 4), owner // 2),
        )

    def product(owner, j, part):
        left = halves[pl.ds(pl.multiple_of(part * nao + j * tile, tile), tile), :]
        return lax.dot_general(
            left, halves[place(owner), :], (((1,), (1,)), ((), ())), preferred_element_type=jnp.float32
        )

    below = lax.broadcasted_iota(jnp.int32, (tile, tile), 0) >= lax.broadcasted_iota(jnp.int32, (tile, tile), 1)

    def diagonal(owner):
        return jnp.where(below, product(owner, owner, 0), product(owner, owner, 1))

    def coded(value, rows_scale, cols_scale):
        return jnp.round(value * rows_scale * cols_scale).astype(jnp.int32).astype(jnp.int16)

    def send_codes(step, unit):
        return remote(
            codes.at[step, unit], codes_in.at[step, unit],
            code_send.at[step, unit], code_recv.at[step, unit], peer(step),
        )

    def send_blocks(step, carry):
        owner = lax.rem(chip + offset(step), 4)
        for unit, (j, part) in enumerate(sources(owner)):
            value = product(owner, j, part)
            codes[step, unit] = coded(value.T, scale_cols[place(owner), :], gain / scales[0:1, place(j)])
            send_codes(step, unit).start()
        return carry

    def send_diagonal(step, carry):
        owner = lax.rem(chip + offset(step), 4)
        value = diagonal(owner)
        codes[step, 3] = coded(value.T, scale_cols[place(owner), :], gain / scales[0:1, place(owner)])
        send_codes(step, 3).start()
        return carry

    lax.fori_loop(0, 3, send_blocks, 0)
    for unit, (j, part) in enumerate(sources(chip)):
        total[unit] = product(chip, j, part).T
    lax.fori_loop(0, 3, send_diagonal, 0)
    total[3] = diagonal(chip).T

    summed = scales[...] * scales[...]
    for step in range(3):
        send_scales(step).wait()
        summed += scales_in[step] * scales_in[step]
        received = scales_in[step, 0:1, place(chip)]
        turned[step] = jnp.broadcast_to(received, (tile, tile)).T * (1.0 / LEVELS)
    sums_scale[...] = jnp.sqrt(summed)
    share_scales().start()
    own_turned = jnp.broadcast_to(sums_scale[0:1, place(chip)], (tile, tile)).T

    def gather(step, unit, j):
        send_codes(step, unit).wait()
        wide = codes_in[step, unit].astype(jnp.int32).astype(jnp.float32)
        total[unit] += wide * turned[step] * scales_in[step, 0:1, place(j)]

    def send_sum(unit, side):
        j = sources(chip)[unit][0]
        return remote(
            sums.at[unit, pl.ds(side * 64, 64)], sums_in.at[core, unit],
            sum_send.at[unit, side], sum_recv.at[core, unit], (kpt, j * 2 + side),
        )

    def take_sum(k, unit):
        return remote(
            sums.at[unit, pl.ds(0, 64)], sums_in.at[k, unit], sum_send.at[unit, 0], sum_recv.at[k, unit], here
        )

    for unit, (j, part) in enumerate(sources(chip)):
        for step in range(3):
            gather(step, unit, j)
        sums[unit] = coded(
            (total[unit] * (gain / own_turned) * (gain / sums_scale[0:1, place(j)])).T, 1.0, 1.0
        )
        for side in range(2):
            send_sum(unit, side).start()

    def hand(unit, part, j):
        return remote(
            handed.at[unit], out.at[core, part, :, place(j)], hand_send.at[unit], hand_recv.at[unit], here
        )

    mine = pl.ds(pl.multiple_of(core * 64, 64), 64)
    theirs = pl.ds(pl.multiple_of((1 - core) * 64, 64), 64)
    final = [(unit, part, j) for unit, (j, part) in enumerate(sources(chip))]
    final += [(3, 0, chip), (4, 1, chip)]
    for unit, part, j in final[:3]:
        handed[unit] = total[unit, theirs, :] * factor
        hand(unit, part, j).start()
        out[core, part, :, place(j)] = total[unit, mine, :] * factor
    for step in range(3):
        gather(step, 3, chip)
    packed = total[3] * factor
    turned[0] = packed.T
    strict = lax.broadcasted_iota(jnp.int32, (tile, tile), 0) > lax.broadcasted_iota(jnp.int32, (tile, tile), 1)
    real = jnp.where(strict, turned[0], packed)
    imag = jnp.where(strict, packed, 0.0)
    total[3] = real
    total[4] = imag - imag.T
    for unit, part, j in final[3:]:
        handed[unit] = total[unit, theirs, :]
        hand(unit, part, j).start()
        out[core, part, :, place(j)] = total[unit, mine, :]

    share_scales().wait()
    for same in range(2):
        k = core if same == 1 else 1 - core
        scale = sums_scale if same == 1 else other_scale
        block_rows = jnp.broadcast_to(scale[0:1, place(chip)], (tile, tile)).T * (factor / LEVELS)
        turned[same] = block_rows
        down = turned[same, mine, :]
        for unit, (j, part) in enumerate(
            ((lax.rem(chip + 3, 4), 0), (lax.rem(chip + 1, 4), 1), (lax.rem(chip + 2, 4), 1 - chip // 2))
        ):
            take_sum(k, unit).wait_recv()
            wide = sums_in[k, unit].astype(jnp.int32).astype(jnp.float32)
            sign = 1 - 2 * part
            value = wide * down * scale[0:1, place(j)]
            out[k, part, :, place(j)] = value * jnp.float32(sign) if isinstance(part, int) else value * sign.astype(jnp.float32)

    for unit in range(3):
        for side in range(2):
            send_sum(unit, side).wait_send()
    for unit, part, j in final:
        hand(unit, part, j).wait()
    for q in range(2):
        for t in range(PIECES):
            for part in range(2):
                x_piece(q, t, part).wait_send()
            relay(q, t).wait_send()
        for r in range(2):
            share(r, q).wait_send()
    for r in range(2):
        for p in range(naux):
            given_pair(r, p).wait_send()


def body(pairs, orbs, match):
    rounds, per_device, naux, nao, _ = pairs.shape
    nocc = orbs.shape[2] // 2
    factor = 1.0 / (rounds * naux * lax.axis_size("aux") * nocc) ** 0.5
    dma = pltpu.SemaphoreType.DMA
    combos = 2 * naux
    orbital_chunk = pltpu.VMEM((per_device, nao, nocc), jnp.bfloat16)
    return pl.pallas_call(
        functools.partial(kernel, factor),
        out_shape=jax.ShapeDtypeStruct((per_device, 2, nao // 8, nao), jnp.float32),
        in_specs=[
            pl.BlockSpec(memory_space=pl.ANY),
            pl.BlockSpec(memory_space=pl.ANY),
            pl.BlockSpec(memory_space=pltpu.SMEM),
        ],
        out_specs=pl.BlockSpec(memory_space=pltpu.VMEM),
        scratch_shapes=[
            pltpu.VMEM((rounds, combos, nao, 2 * nao), jnp.bfloat16),
            orbital_chunk, orbital_chunk, orbital_chunk, orbital_chunk,
            pltpu.VMEM((2 * nao, nocc), jnp.bfloat16),
            pltpu.VMEM((2 * nao, rounds * combos * 2 * nocc), jnp.bfloat16),
            pltpu.VMEM((nao, 128), jnp.float32),
            pltpu.VMEM((nao, 128), jnp.float32),
            pltpu.VMEM((3, 4, 128, 128), jnp.int16),
            pltpu.VMEM((3, 4, 128, 128), jnp.int16),
            pltpu.VMEM((8, nao), jnp.float32),
            pltpu.VMEM((3, 8, nao), jnp.float32),
            pltpu.VMEM((8, nao), jnp.float32),
            pltpu.VMEM((8, nao), jnp.float32),
            pltpu.VMEM((3, 128, 128), jnp.float32),
            pltpu.VMEM((5, 128, 128), jnp.float32),
            pltpu.VMEM((3, 128, 128), jnp.int16),
            pltpu.VMEM((2, 3, 64, 128), jnp.int16),
            pltpu.VMEM((5, 64, 128), jnp.float32),
            dma((rounds, naux)), dma((rounds, naux)), dma((rounds, naux)),
            dma((2, PIECES, 2)), dma((2, PIECES, 2)), dma((2, PIECES)), dma((2, PIECES)),
            dma((2, 2)), dma((2, 2)), dma((3, 4)), dma((3, 4)), dma((3,)), dma((3,)), dma((2,)),
            dma((3, 2)), dma((2, 3)), dma((5,)), dma((5,)),
        ],
        compiler_params=pltpu.CompilerParams(
            collective_id=0, has_side_effects=True, vmem_limit_bytes=56 << 20
        ),
    )(pairs, orbs, match)


def solution(mesh):
    placed = (P(None, "kpt", "aux", None, None), P("kpt", None, None), P())
    return jax.shard_map(
        body, mesh=mesh, in_specs=placed, out_specs=P("kpt", None, "aux", None), check_vma=False
    )
```

```python
import functools

import jax
import jax.numpy as jnp
from jax import lax
from jax.experimental import pallas as pl
from jax.experimental.pallas import tpu as pltpu
from jax.sharding import PartitionSpec as P

MESH = pl.DeviceIdType.MESH
ROUNDS = 2
LEVELS = 32000.0
SMALLEST = 1e-30
PIECES = (
    ((0, 64), (64, 64), (128, 128), (256, 128), (384, 128)),
    ((0, 128), (128, 128), (256, 128), (384, 64), (448, 64)),
)
MOST = 5


def kernel(
    factor, pairs, orbs, match, out,
    held_pairs, own_orbs, staged, c00, c01, c10, c11, block, halves, squares, scale_cols,
    codes, codes_in, scales, scales_in, sums_scale, other_scale, turned, total, sums, sums_in, handed,
    stage_sem, pair_sem, pair_send, pair_recv, x_send, x_recv, relay_send, relay_recv,
    share_send, share_recv, code_send, code_recv, scale_send, scale_recv, share_scale_sem,
    sum_send, sum_recv, hand_send, hand_recv,
):
    kpt, aux = lax.axis_index("kpt"), lax.axis_index("aux")
    chip, core = aux // 2, aux % 2
    x = kpt // 8
    rest = kpt - x * 8
    near = (x + 1 - 2 * (x % 2)) * 8 + rest
    far = (x + 2 - 4 * (x // 2)) * 8 + rest
    cross = (3 - x) * 8 + rest
    sibling = aux + 1 - 2 * core
    here = (kpt, sibling)
    nao, nocc = orbs.shape[1], orbs.shape[2] // 2
    width = nocc // 2
    naux = pairs.shape[2]
    tile = nao // 4
    combos = 2 * naux
    far_chunks, near_chunks = (c00, c01), (c10, c11)

    def remote(src, dst, send, recv, device):
        return pltpu.make_async_remote_copy(
            src_ref=src, dst_ref=dst, send_sem=send, recv_sem=recv, device_id=device, device_id_type=MESH
        )

    def own_pair(r, p):
        return pltpu.make_async_copy(
            pairs.at[r, core, p], held_pairs.at[r, core * naux + p], pair_sem.at[r, p]
        )

    def given_pair(r, p):
        return remote(
            pairs.at[r, 1 - core, p], held_pairs.at[r, core * naux + p],
            pair_send.at[r, p], pair_recv.at[r, p], here,
        )

    def stage(k):
        return pltpu.make_async_copy(orbs.at[k], own_orbs.at[k], stage_sem.at[k])

    def part_of(q, t):
        return pl.ds(*PIECES[q][t])

    def x_piece(q, t):
        return remote(
            staged.at[q, part_of(q, t)], near_chunks[q].at[core, part_of(q, t)],
            x_send.at[q, t], x_recv.at[q, t], (near, aux),
        )

    def relay(q, t):
        return remote(
            near_chunks[q].at[core, part_of(q, t)], far_chunks[q].at[part_of(q, t)],
            relay_send.at[q, t], relay_recv.at[q, t], (cross, aux),
        )

    def share(q, t):
        piece = near_chunks[q].at[core, part_of(q, t)]
        return remote(piece, piece, share_send.at[q, t], share_recv.at[q, t], here)

    def within(r, block, k):
        return jnp.bitwise_and(match[r, block * 2 + k], 1)

    for k in range(2):
        stage(k).start()
    for r in (1, 0):
        for p in range(naux):
            own_pair(r, p).start()

    barrier = pltpu.get_barrier_semaphore()
    peers = [(kpt, lax.rem(chip + d, 4) * 2 + side) for d in (1, 2, 3) for side in range(2)]
    for device in [(near, aux), (cross, aux), here] + peers:
        pl.semaphore_signal(barrier, inc=1, device_id=device, device_id_type=MESH)
    for k in range(2):
        stage(k).wait()
    index = within(0, far, core)
    for q in range(2):
        for part in range(2):
            staged[q, :, part * width : (part + 1) * width] = own_orbs[
                index, :, part * nocc + q * width : part * nocc + (q + 1) * width
            ]

    pl.semaphore_wait(barrier, 9)

    for q in range(2):
        for t in range(MOST):
            x_piece(q, t).start()
    for r in (1, 0):
        for p in range(naux):
            given_pair(r, p).start()
    squares[...] = jnp.zeros_like(squares)

    def pass_on(q, t):
        x_piece(q, t).wait_recv()
        relay(q, t).start()
        share(q, t).start()

    def build(r, q):
        if r == 0:
            both = far_chunks[q][...]
        else:
            both = near_chunks[q][jnp.bitwise_xor(within(0, cross, 0), within(1, kpt, core))]
        block[0:nao, :] = both
        block[nao:, 0:width] = -both[:, width:]
        block[nao:, width:] = both[:, 0:width]

    def transform(r, q, first, last):
        def step(p):
            done = jnp.dot(held_pairs[r, p], block[...], preferred_element_type=jnp.float32).astype(jnp.bfloat16)
            real, imag = done[:, 0:width], done[:, width:]
            at = (r * combos + p) * 2 * nocc + q * 2 * width
            halves[0:nao, pl.ds(at, 2 * width)] = done
            halves[nao:, pl.ds(at, 2 * width)] = jnp.concatenate([-imag, real], axis=1)
            wide_real, wide_imag = real.astype(jnp.float32), imag.astype(jnp.float32)
            squares[...] += wide_real * wide_real + wide_imag * wide_imag

        for p in range(first, last):
            step(p)

    def pairs_of(r):
        for p in range(naux):
            own_pair(r, p).wait()
        for p in range(naux):
            given_pair(r, p).wait_recv()

    def near_here(q):
        for t in range(MOST):
            share(q, t).wait_recv()
        build(1, q)

    def far_here(q):
        for t in range(MOST):
            relay(q, t).wait_recv()
        build(0, q)

    for t in range(MOST):
        pass_on(0, t)
    pairs_of(1)
    near_here(0)
    transform(1, 0, 0, 1)
    pass_on(1, 0)
    transform(1, 0, 1, 4)
    pass_on(1, 1)
    pairs_of(0)
    far_here(0)
    transform(0, 0, 0, 3)
    pass_on(1, 2)
    transform(0, 0, 3, 4)
    pass_on(1, 3)
    pass_on(1, 4)
    near_here(1)
    transform(1, 1, 0, 4)
    far_here(1)
    transform(0, 1, 0, 4)

    gain = LEVELS ** 0.5
    length = jnp.sqrt(jnp.maximum(jnp.sum(squares[...], axis=1, keepdims=True), SMALLEST))
    spread = jnp.broadcast_to(length, (nao, tile))
    scale_cols[...] = gain / spread
    for j in range(4):
        scales[:, j * tile : (j + 1) * tile] = spread[j * tile : (j + 1) * tile, :].T[0:8, :]

    def place(j):
        return pl.ds(pl.multiple_of(lax.rem(j, 4) * tile, tile), tile)

    def offset(step):
        return 2 - step + 3 * (step // 2)

    def peer(step):
        return (kpt, lax.rem(chip + offset(step), 4) * 2 + core)

    def send_scales(step):
        return remote(scales, scales_in.at[step], scale_send.at[step], scale_recv.at[step], peer(step))

    def share_scales():
        return remote(sums_scale, other_scale, share_scale_sem.at[0], share_scale_sem.at[1], here)

    for step in range(3):
        send_scales(step).start()

    def sources(owner):
        return (
            (lax.rem(owner + 1, 4), 0), (lax.rem(owner + 3, 4), 1), (lax.rem(owner + 2, 4), owner // 2),
        )

    def product(owner, j, part):
        left = halves[pl.ds(pl.multiple_of(part * nao + j * tile, tile), tile), :]
        return lax.dot_general(
            left, halves[place(owner), :], (((1,), (1,)), ((), ())), preferred_element_type=jnp.float32
        )

    below = lax.broadcasted_iota(jnp.int32, (tile, tile), 0) >= lax.broadcasted_iota(jnp.int32, (tile, tile), 1)

    def diagonal(owner):
        return jnp.where(below, product(owner, owner, 0), product(owner, owner, 1))

    def coded(value, rows_scale, cols_scale):
        return jnp.round(value * rows_scale * cols_scale).astype(jnp.int32).astype(jnp.int16)

    def send_codes(step, unit):
        return remote(
            codes.at[step, unit], codes_in.at[step, unit],
            code_send.at[step, unit], code_recv.at[step, unit], peer(step),
        )

    def send_unit(unit, step, carry):
        owner = lax.rem(chip + offset(step), 4)
        if unit == 3:
            j, value = owner, diagonal(owner)
        else:
            j, part = sources(owner)[unit]
            value = product(owner, j, part)
        codes[step, unit] = coded(value.T, scale_cols[place(owner), :], gain / scales[0:1, place(j)])
        send_codes(step, unit).start()
        return carry

    order = (2, 0, 1)
    for unit in order + (3,):
        lax.fori_loop(0, 3, functools.partial(send_unit, unit), 0)
    for unit in order:
        j, part = sources(chip)[unit]
        total[unit] = product(chip, j, part).T
    total[3] = diagonal(chip).T

    summed = scales[...] * scales[...]
    for step in range(3):
        send_scales(step).wait()
        summed += scales_in[step] * scales_in[step]
        received = scales_in[step, 0:1, place(chip)]
        turned[step] = jnp.broadcast_to(received, (tile, tile)).T * (1.0 / LEVELS)
    sums_scale[...] = jnp.sqrt(summed)
    share_scales().start()
    own_turned = jnp.broadcast_to(sums_scale[0:1, place(chip)], (tile, tile)).T

    def gather(step, unit, j):
        send_codes(step, unit).wait()
        wide = codes_in[step, unit].astype(jnp.int32).astype(jnp.float32)
        total[unit] += wide * turned[step] * scales_in[step, 0:1, place(j)]

    def send_sum(unit, side):
        j = sources(chip)[unit][0]
        return remote(
            sums.at[unit, pl.ds(side * 64, 64)], sums_in.at[core, unit],
            sum_send.at[unit, side], sum_recv.at[core, unit], (kpt, j * 2 + side),
        )

    def take_sum(k, unit):
        return remote(
            sums.at[unit, pl.ds(0, 64)], sums_in.at[k, unit], sum_send.at[unit, 0], sum_recv.at[k, unit], here
        )

    for unit in order:
        j = sources(chip)[unit][0]
        for step in range(3):
            gather(step, unit, j)
        sums[unit] = coded(
            (total[unit] * (gain / own_turned) * (gain / sums_scale[0:1, place(j)])).T, 1.0, 1.0
        )
        for side in range(2):
            send_sum(unit, side).start()

    def hand(unit, part, j):
        return remote(
            handed.at[unit], out.at[core, part, :, place(j)], hand_send.at[unit], hand_recv.at[unit], here
        )

    mine = pl.ds(pl.multiple_of(core * 64, 64), 64)
    theirs = pl.ds(pl.multiple_of((1 - core) * 64, 64), 64)
    final = [(unit, part, j) for unit, (j, part) in enumerate(sources(chip))]
    final += [(3, 0, chip), (4, 1, chip)]
    for unit, part, j in final[:3]:
        handed[unit] = total[unit, theirs, :] * factor
        hand(unit, part, j).start()
        out[core, part, :, place(j)] = total[unit, mine, :] * factor
    for step in range(3):
        gather(step, 3, chip)
    packed = total[3] * factor
    turned[0] = packed.T
    strict = lax.broadcasted_iota(jnp.int32, (tile, tile), 0) > lax.broadcasted_iota(jnp.int32, (tile, tile), 1)
    real = jnp.where(strict, turned[0], packed)
    imag = jnp.where(strict, packed, 0.0)
    total[3] = real
    total[4] = imag - imag.T
    for unit, part, j in final[3:]:
        handed[unit] = total[unit, theirs, :]
        hand(unit, part, j).start()
        out[core, part, :, place(j)] = total[unit, mine, :]

    share_scales().wait()
    for same in range(2):
        k = core if same == 1 else 1 - core
        scale = sums_scale if same == 1 else other_scale
        block_rows = jnp.broadcast_to(scale[0:1, place(chip)], (tile, tile)).T * (factor / LEVELS)
        turned[same] = block_rows
        down = turned[same, mine, :]
        for unit, (j, part) in enumerate(
            ((lax.rem(chip + 3, 4), 0), (lax.rem(chip + 1, 4), 1), (lax.rem(chip + 2, 4), 1 - chip // 2))
        ):
            take_sum(k, unit).wait_recv()
            wide = sums_in[k, unit].astype(jnp.int32).astype(jnp.float32)
            sign = 1 - 2 * part
            value = wide * down * scale[0:1, place(j)]
            out[k, part, :, place(j)] = value * jnp.float32(sign) if isinstance(part, int) else value * sign.astype(jnp.float32)

    for unit in range(3):
        for side in range(2):
            send_sum(unit, side).wait_send()
    for unit, part, j in final:
        hand(unit, part, j).wait()
    for q in range(2):
        for t in range(MOST):
            x_piece(q, t).wait_send()
            relay(q, t).wait_send()
            share(q, t).wait_send()
    for r in range(2):
        for p in range(naux):
            given_pair(r, p).wait_send()


def body(pairs, orbs, match):
    rounds, per_device, naux, nao, _ = pairs.shape
    nocc = orbs.shape[2] // 2
    factor = 1.0 / (rounds * naux * lax.axis_size("aux") * nocc) ** 0.5
    dma = pltpu.SemaphoreType.DMA
    combos = 2 * naux
    far_chunk = pltpu.VMEM((nao, nocc), jnp.bfloat16)
    near_chunk = pltpu.VMEM((per_device, nao, nocc), jnp.bfloat16)
    return pl.pallas_call(
        functools.partial(kernel, factor),
        out_shape=jax.ShapeDtypeStruct((per_device, 2, nao // 8, nao), jnp.float32),
        in_specs=[
            pl.BlockSpec(memory_space=pl.ANY),
            pl.BlockSpec(memory_space=pl.ANY),
            pl.BlockSpec(memory_space=pltpu.SMEM),
        ],
        out_specs=pl.BlockSpec(memory_space=pltpu.VMEM),
        scratch_shapes=[
            pltpu.VMEM((rounds, combos, nao, 2 * nao), jnp.bfloat16),
            pltpu.VMEM((per_device, nao, 2 * nocc), jnp.bfloat16),
            pltpu.VMEM((2, nao, nocc), jnp.bfloat16),
            far_chunk, far_chunk, near_chunk, near_chunk,
            pltpu.VMEM((2 * nao, nocc), jnp.bfloat16),
            pltpu.VMEM((2 * nao, rounds * combos * 2 * nocc), jnp.bfloat16),
            pltpu.VMEM((nao, 128), jnp.float32),
            pltpu.VMEM((nao, 128), jnp.float32),
            pltpu.VMEM((3, 4, 128, 128), jnp.int16),
            pltpu.VMEM((3, 4, 128, 128), jnp.int16),
            pltpu.VMEM((8, nao), jnp.float32),
            pltpu.VMEM((3, 8, nao), jnp.float32),
            pltpu.VMEM((8, nao), jnp.float32),
            pltpu.VMEM((8, nao), jnp.float32),
            pltpu.VMEM((3, 128, 128), jnp.float32),
            pltpu.VMEM((5, 128, 128), jnp.float32),
            pltpu.VMEM((3, 128, 128), jnp.int16),
            pltpu.VMEM((2, 3, 64, 128), jnp.int16),
            pltpu.VMEM((5, 64, 128), jnp.float32),
            dma((per_device,)), dma((rounds, naux)), dma((rounds, naux)), dma((rounds, naux)),
            dma((2, MOST)), dma((2, MOST)), dma((2, MOST)), dma((2, MOST)),
            dma((2, MOST)), dma((2, MOST)), dma((3, 4)), dma((3, 4)), dma((3,)), dma((3,)), dma((2,)),
            dma((3, 2)), dma((2, 3)), dma((5,)), dma((5,)),
        ],
        compiler_params=pltpu.CompilerParams(
            collective_id=0, has_side_effects=True, vmem_limit_bytes=56 << 20
        ),
    )(pairs, orbs, match)


def solution(mesh):
    placed = (P(None, "kpt", "aux", None, None), P("kpt", None, None), P())
    return jax.shard_map(
        body, mesh=mesh, in_specs=placed, out_specs=P("kpt", None, "aux", None), check_vma=False
    )
```

```python
import functools

import jax
import jax.numpy as jnp
from jax import lax
from jax.experimental import pallas as pl
from jax.experimental.pallas import tpu as pltpu
from jax.sharding import PartitionSpec as P

MESH = pl.DeviceIdType.MESH
ROUNDS = 2
LEVELS = 32000.0
SMALLEST = 1e-30
PIECES = (
    ((0, 64), (64, 64), (128, 128), (256, 128), (384, 128)),
    ((0, 128), (128, 128), (256, 128), (384, 64), (448, 64)),
)
MOST = 5


def kernel(
    factor, pairs, orbs, match_far, out,
    match, match_sem, held_pairs, own_orbs, staged, c00, c01, c10, c11, block, halves, squares, scale_cols,
    codes, codes_in, scales, scales_in, sums_scale, other_scale, turned, total, sums, sums_in, handed,
    stage_sem, pair_sem, pair_send, pair_recv, x_send, x_recv, relay_send, relay_recv,
    share_send, share_recv, code_send, code_recv, scale_send, scale_recv, share_scale_sem,
    sum_send, sum_recv, hand_send, hand_recv,
):
    kpt, aux = lax.axis_index("kpt"), lax.axis_index("aux")
    chip, core = aux // 2, aux % 2
    x = kpt // 8
    rest = kpt - x * 8
    near = (x + 1 - 2 * (x % 2)) * 8 + rest
    far = (x + 2 - 4 * (x // 2)) * 8 + rest
    cross = (3 - x) * 8 + rest
    sibling = aux + 1 - 2 * core
    here = (kpt, sibling)
    nao, nocc = orbs.shape[1], orbs.shape[2] // 2
    width = nocc // 2
    naux = pairs.shape[2]
    tile = nao // 4
    combos = 2 * naux
    far_chunks, near_chunks = (c00, c01), (c10, c11)

    def remote(src, dst, send, recv, device):
        return pltpu.make_async_remote_copy(
            src_ref=src, dst_ref=dst, send_sem=send, recv_sem=recv, device_id=device, device_id_type=MESH
        )

    def own_pair(r, p):
        return pltpu.make_async_copy(
            pairs.at[r, core, p], held_pairs.at[r, core * naux + p], pair_sem.at[r, p]
        )

    def given_pair(r, p):
        return remote(
            pairs.at[r, 1 - core, p], held_pairs.at[r, core * naux + p],
            pair_send.at[r, p], pair_recv.at[r, p], here,
        )

    def stage(k):
        return pltpu.make_async_copy(orbs.at[k], own_orbs.at[k], stage_sem.at[k])

    def part_of(q, t):
        return pl.ds(*PIECES[q][t])

    def x_piece(q, t):
        return remote(
            staged.at[q, part_of(q, t)], near_chunks[q].at[core, part_of(q, t)],
            x_send.at[q, t], x_recv.at[q, t], (near, aux),
        )

    def relay(q, t):
        return remote(
            near_chunks[q].at[core, part_of(q, t)], far_chunks[q].at[part_of(q, t)],
            relay_send.at[q, t], relay_recv.at[q, t], (cross, aux),
        )

    def share(q, t):
        piece = near_chunks[q].at[core, part_of(q, t)]
        return remote(piece, piece, share_send.at[q, t], share_recv.at[q, t], here)

    def within(r, block, k):
        return jnp.bitwise_and(match[r, block * 2 + k], 1)

    indices = pltpu.make_async_copy(match_far, match, match_sem)
    indices.start()
    for k in range(2):
        stage(k).start()
    for r in (1, 0):
        for p in range(naux):
            own_pair(r, p).start()

    barrier = pltpu.get_barrier_semaphore()
    peers = [(kpt, lax.rem(chip + d, 4) * 2 + side) for d in (1, 2, 3) for side in range(2)]
    for device in [(near, aux), (cross, aux), here] + peers:
        pl.semaphore_signal(barrier, inc=1, device_id=device, device_id_type=MESH)
    for k in range(2):
        stage(k).wait()
    indices.wait()
    index = within(0, far, core)
    for q in range(2):
        for part in range(2):
            staged[q, :, part * width : (part + 1) * width] = own_orbs[
                index, :, part * nocc + q * width : part * nocc + (q + 1) * width
            ]

    pl.semaphore_wait(barrier, 9)

    for q in range(2):
        for t in range(MOST):
            x_piece(q, t).start()
    for r in (1, 0):
        for p in range(naux):
            given_pair(r, p).start()
    squares[...] = jnp.zeros_like(squares)

    def pass_on(q, t):
        x_piece(q, t).wait_recv()
        relay(q, t).start()
        share(q, t).start()

    def build(r, q):
        if r == 0:
            both = far_chunks[q][...]
        else:
            both = near_chunks[q][jnp.bitwise_xor(within(0, cross, 0), within(1, kpt, core))]
        block[0:nao, :] = both
        block[nao:, 0:width] = -both[:, width:]
        block[nao:, width:] = both[:, 0:width]

    def transform(r, q, first, last):
        def step(p):
            done = jnp.dot(held_pairs[r, p], block[...], preferred_element_type=jnp.float32).astype(jnp.bfloat16)
            real, imag = done[:, 0:width], done[:, width:]
            at = (r * combos + p) * 2 * nocc + q * 2 * width
            halves[0:nao, pl.ds(at, 2 * width)] = done
            halves[nao:, pl.ds(at, 2 * width)] = jnp.concatenate([-imag, real], axis=1)
            wide_real, wide_imag = real.astype(jnp.float32), imag.astype(jnp.float32)
            squares[...] += wide_real * wide_real + wide_imag * wide_imag

        for p in range(first, last):
            step(p)

    def pairs_of(r):
        for p in range(naux):
            own_pair(r, p).wait()
        for p in range(naux):
            given_pair(r, p).wait_recv()

    def near_here(q):
        for t in range(MOST):
            share(q, t).wait_recv()
        build(1, q)

    def far_here(q):
        for t in range(MOST):
            relay(q, t).wait_recv()
        build(0, q)

    for t in range(MOST):
        pass_on(0, t)
    pairs_of(1)
    near_here(0)
    transform(1, 0, 0, 1)
    pass_on(1, 0)
    transform(1, 0, 1, 4)
    pass_on(1, 1)
    pairs_of(0)
    far_here(0)
    transform(0, 0, 0, 3)
    pass_on(1, 2)
    transform(0, 0, 3, 4)
    pass_on(1, 3)
    pass_on(1, 4)
    near_here(1)
    transform(1, 1, 0, 4)
    far_here(1)
    transform(0, 1, 0, 4)

    gain = LEVELS ** 0.5
    length = jnp.sqrt(jnp.maximum(jnp.sum(squares[...], axis=1, keepdims=True), SMALLEST))
    spread = jnp.broadcast_to(length, (nao, tile))
    scale_cols[...] = gain / spread
    for j in range(4):
        scales[:, j * tile : (j + 1) * tile] = spread[j * tile : (j + 1) * tile, :].T[0:8, :]

    def place(j):
        return pl.ds(pl.multiple_of(lax.rem(j, 4) * tile, tile), tile)

    def offset(step):
        return 2 - step + 3 * (step // 2)

    def peer(step):
        return (kpt, lax.rem(chip + offset(step), 4) * 2 + core)

    def send_scales(step):
        return remote(scales, scales_in.at[step], scale_send.at[step], scale_recv.at[step], peer(step))

    def share_scales():
        return remote(sums_scale, other_scale, share_scale_sem.at[0], share_scale_sem.at[1], here)

    for step in range(3):
        send_scales(step).start()

    def sources(owner):
        return (
            (lax.rem(owner + 1, 4), 0), (lax.rem(owner + 3, 4), 1), (lax.rem(owner + 2, 4), owner // 2),
        )

    def product(owner, j, part):
        left = halves[pl.ds(pl.multiple_of(part * nao + j * tile, tile), tile), :]
        return lax.dot_general(
            left, halves[place(owner), :], (((1,), (1,)), ((), ())), preferred_element_type=jnp.float32
        )

    below = lax.broadcasted_iota(jnp.int32, (tile, tile), 0) >= lax.broadcasted_iota(jnp.int32, (tile, tile), 1)

    def diagonal(owner):
        return jnp.where(below, product(owner, owner, 0), product(owner, owner, 1))

    def coded(value, rows_scale, cols_scale):
        return jnp.round(value * rows_scale * cols_scale).astype(jnp.int32).astype(jnp.int16)

    def send_codes(step, unit):
        return remote(
            codes.at[step, unit], codes_in.at[step, unit],
            code_send.at[step, unit], code_recv.at[step, unit], peer(step),
        )

    def send_unit(unit, step, carry):
        owner = lax.rem(chip + offset(step), 4)
        if unit == 3:
            j, value = owner, diagonal(owner)
        else:
            j, part = sources(owner)[unit]
            value = product(owner, j, part)
        codes[step, unit] = coded(value.T, scale_cols[place(owner), :], gain / scales[0:1, place(j)])
        send_codes(step, unit).start()
        return carry

    order = (2, 0, 1)
    for unit in order + (3,):
        lax.fori_loop(0, 3, functools.partial(send_unit, unit), 0)
    for unit in order:
        j, part = sources(chip)[unit]
        total[unit] = product(chip, j, part).T
    total[3] = diagonal(chip).T

    summed = scales[...] * scales[...]
    for step in range(3):
        send_scales(step).wait()
        summed += scales_in[step] * scales_in[step]
        received = scales_in[step, 0:1, place(chip)]
        turned[step] = jnp.broadcast_to(received, (tile, tile)).T * (1.0 / LEVELS)
    sums_scale[...] = jnp.sqrt(summed)
    share_scales().start()
    own_turned = jnp.broadcast_to(sums_scale[0:1, place(chip)], (tile, tile)).T

    def gather(step, unit, j):
        send_codes(step, unit).wait()
        wide = codes_in[step, unit].astype(jnp.int32).astype(jnp.float32)
        total[unit] += wide * turned[step] * scales_in[step, 0:1, place(j)]

    def send_sum(unit, side):
        j = sources(chip)[unit][0]
        return remote(
            sums.at[unit, pl.ds(side * 64, 64)], sums_in.at[core, unit],
            sum_send.at[unit, side], sum_recv.at[core, unit], (kpt, j * 2 + side),
        )

    def take_sum(k, unit):
        return remote(
            sums.at[unit, pl.ds(0, 64)], sums_in.at[k, unit], sum_send.at[unit, 0], sum_recv.at[k, unit], here
        )

    for unit in order:
        j = sources(chip)[unit][0]
        for step in range(3):
            gather(step, unit, j)
        sums[unit] = coded(
            (total[unit] * (gain / own_turned) * (gain / sums_scale[0:1, place(j)])).T, 1.0, 1.0
        )
        for side in range(2):
            send_sum(unit, side).start()

    def hand(unit, part, j):
        return remote(
            handed.at[unit], out.at[core, part, :, place(j)], hand_send.at[unit], hand_recv.at[unit], here
        )

    mine = pl.ds(pl.multiple_of(core * 64, 64), 64)
    theirs = pl.ds(pl.multiple_of((1 - core) * 64, 64), 64)
    final = [(unit, part, j) for unit, (j, part) in enumerate(sources(chip))]
    final += [(3, 0, chip), (4, 1, chip)]
    for unit, part, j in final[:3]:
        handed[unit] = total[unit, theirs, :] * factor
        hand(unit, part, j).start()
        out[core, part, :, place(j)] = total[unit, mine, :] * factor
    for step in range(3):
        gather(step, 3, chip)
    packed = total[3] * factor
    turned[0] = packed.T
    strict = lax.broadcasted_iota(jnp.int32, (tile, tile), 0) > lax.broadcasted_iota(jnp.int32, (tile, tile), 1)
    real = jnp.where(strict, turned[0], packed)
    imag = jnp.where(strict, packed, 0.0)
    total[3] = real
    total[4] = imag - imag.T
    for unit, part, j in final[3:]:
        handed[unit] = total[unit, theirs, :]
        hand(unit, part, j).start()
        out[core, part, :, place(j)] = total[unit, mine, :]

    share_scales().wait()
    for same in range(2):
        k = core if same == 1 else 1 - core
        scale = sums_scale if same == 1 else other_scale
        block_rows = jnp.broadcast_to(scale[0:1, place(chip)], (tile, tile)).T * (factor / LEVELS)
        turned[same] = block_rows
        down = turned[same, mine, :]
        for unit, (j, part) in enumerate(
            ((lax.rem(chip + 3, 4), 0), (lax.rem(chip + 1, 4), 1), (lax.rem(chip + 2, 4), 1 - chip // 2))
        ):
            take_sum(k, unit).wait_recv()
            wide = sums_in[k, unit].astype(jnp.int32).astype(jnp.float32)
            sign = 1 - 2 * part
            value = wide * down * scale[0:1, place(j)]
            out[k, part, :, place(j)] = value * jnp.float32(sign) if isinstance(part, int) else value * sign.astype(jnp.float32)

    for unit in range(3):
        for side in range(2):
            send_sum(unit, side).wait_send()
    for unit, part, j in final:
        hand(unit, part, j).wait()
    for q in range(2):
        for t in range(MOST):
            x_piece(q, t).wait_send()
            relay(q, t).wait_send()
            share(q, t).wait_send()
    for r in range(2):
        for p in range(naux):
            given_pair(r, p).wait_send()


def body(pairs, orbs, match):
    rounds, per_device, naux, nao, _ = pairs.shape
    nocc = orbs.shape[2] // 2
    factor = 1.0 / (rounds * naux * lax.axis_size("aux") * nocc) ** 0.5
    dma = pltpu.SemaphoreType.DMA
    combos = 2 * naux
    far_chunk = pltpu.VMEM((nao, nocc), jnp.bfloat16)
    near_chunk = pltpu.VMEM((per_device, nao, nocc), jnp.bfloat16)
    return pl.pallas_call(
        functools.partial(kernel, factor),
        out_shape=jax.ShapeDtypeStruct((per_device, 2, nao // 8, nao), jnp.float32),
        in_specs=[
            pl.BlockSpec(memory_space=pl.ANY),
            pl.BlockSpec(memory_space=pl.ANY),
            pl.BlockSpec(memory_space=pl.ANY),
        ],
        out_specs=pl.BlockSpec(memory_space=pltpu.VMEM),
        scratch_shapes=[
            pltpu.SMEM((2, 64), jnp.int32), dma,
            pltpu.VMEM((rounds, combos, nao, 2 * nao), jnp.bfloat16),
            pltpu.VMEM((per_device, nao, 2 * nocc), jnp.bfloat16),
            pltpu.VMEM((2, nao, nocc), jnp.bfloat16),
            far_chunk, far_chunk, near_chunk, near_chunk,
            pltpu.VMEM((2 * nao, nocc), jnp.bfloat16),
            pltpu.VMEM((2 * nao, rounds * combos * 2 * nocc), jnp.bfloat16),
            pltpu.VMEM((nao, 128), jnp.float32),
            pltpu.VMEM((nao, 128), jnp.float32),
            pltpu.VMEM((3, 4, 128, 128), jnp.int16),
            pltpu.VMEM((3, 4, 128, 128), jnp.int16),
            pltpu.VMEM((8, nao), jnp.float32),
            pltpu.VMEM((3, 8, nao), jnp.float32),
            pltpu.VMEM((8, nao), jnp.float32),
            pltpu.VMEM((8, nao), jnp.float32),
            pltpu.VMEM((3, 128, 128), jnp.float32),
            pltpu.VMEM((5, 128, 128), jnp.float32),
            pltpu.VMEM((3, 128, 128), jnp.int16),
            pltpu.VMEM((2, 3, 64, 128), jnp.int16),
            pltpu.VMEM((5, 64, 128), jnp.float32),
            dma((per_device,)), dma((rounds, naux)), dma((rounds, naux)), dma((rounds, naux)),
            dma((2, MOST)), dma((2, MOST)), dma((2, MOST)), dma((2, MOST)),
            dma((2, MOST)), dma((2, MOST)), dma((3, 4)), dma((3, 4)), dma((3,)), dma((3,)), dma((2,)),
            dma((3, 2)), dma((2, 3)), dma((5,)), dma((5,)),
        ],
        compiler_params=pltpu.CompilerParams(
            collective_id=0, has_side_effects=True, vmem_limit_bytes=53 << 20
        ),
    )(pairs, orbs, match)


def solution(mesh):
    placed = (P(None, "kpt", "aux", None, None), P("kpt", None, None), P())
    return jax.shard_map(
        body, mesh=mesh, in_specs=placed, out_specs=P("kpt", None, "aux", None), check_vma=False
    )
```

```python
import functools

import jax
import jax.numpy as jnp
from jax import lax
from jax.experimental import pallas as pl
from jax.experimental.pallas import tpu as pltpu
from jax.sharding import PartitionSpec as P

MESH = pl.DeviceIdType.MESH
ROUNDS = 2
LEVELS = 32000.0
SMALLEST = 1e-30
PIECES = (
    ((0, 64), (64, 64), (128, 128), (256, 128), (384, 128)),
    ((0, 32), (128, 128), (256, 128), (384, 64), (448, 64)),
)
MOST = 5


def kernel(
    factor, pairs, orbs, match_far, out,
    match, match_sem, held_pairs, own_orbs, staged, c00, c01, c10, c11, block, halves, squares, scale_cols,
    codes, codes_in, scales, scales_in, sums_scale, other_scale, turned, total, sums, sums_in, handed,
    stage_sem, pair_sem, pair_send, pair_recv, x_send, x_recv, relay_send, relay_recv, quarter_send, quarter_recv,
    share_send, share_recv, code_send, code_recv, scale_send, scale_recv, share_scale_sem,
    sum_send, sum_recv, hand_send, hand_recv,
):
    kpt, aux = lax.axis_index("kpt"), lax.axis_index("aux")
    chip, core = aux // 2, aux % 2
    x = kpt // 8
    rest = kpt - x * 8
    near = (x + 1 - 2 * (x % 2)) * 8 + rest
    far = (x + 2 - 4 * (x // 2)) * 8 + rest
    cross = (3 - x) * 8 + rest
    sibling = aux + 1 - 2 * core
    here = (kpt, sibling)
    nao, nocc = orbs.shape[1], orbs.shape[2] // 2
    width = nocc // 2
    naux = pairs.shape[2]
    tile = nao // 4
    combos = 2 * naux
    far_chunks, near_chunks = (c00, c01), (c10, c11)

    def remote(src, dst, send, recv, device):
        return pltpu.make_async_remote_copy(
            src_ref=src, dst_ref=dst, send_sem=send, recv_sem=recv, device_id=device, device_id_type=MESH
        )

    def own_pair(r, p):
        return pltpu.make_async_copy(
            pairs.at[r, core, p], held_pairs.at[r, core * naux + p], pair_sem.at[r, p]
        )

    def given_pair(r, p):
        return remote(
            pairs.at[r, 1 - core, p], held_pairs.at[r, core * naux + p],
            pair_send.at[r, p], pair_recv.at[r, p], here,
        )

    def stage(k):
        return pltpu.make_async_copy(orbs.at[k], own_orbs.at[k], stage_sem.at[k])

    def part_of(q, t):
        start, size = PIECES[q][t]
        if (q, t) == (1, 0):
            return pl.ds(pl.multiple_of(chip * size, size), size)
        return pl.ds(start, size)

    def spread_out(r, d):
        piece = (near_chunks[1].at[core] if r else far_chunks[1]).at[part_of(1, 0)]
        return remote(
            piece, piece, quarter_send.at[r, d - 1], quarter_recv.at[r, d - 1],
            (kpt, lax.rem(chip + d, 4) * 2 + core),
        )

    def whole_share():
        piece = near_chunks[1].at[core, pl.ds(0, 128)]
        return remote(piece, piece, share_send.at[1, 0], share_recv.at[1, 0], here)

    def x_piece(q, t):
        return remote(
            staged.at[q, part_of(q, t)], near_chunks[q].at[core, part_of(q, t)],
            x_send.at[q, t], x_recv.at[q, t], (near, aux),
        )

    def relay(q, t):
        return remote(
            near_chunks[q].at[core, part_of(q, t)], far_chunks[q].at[part_of(q, t)],
            relay_send.at[q, t], relay_recv.at[q, t], (cross, aux),
        )

    def share(q, t):
        piece = near_chunks[q].at[core, part_of(q, t)]
        return remote(piece, piece, share_send.at[q, t], share_recv.at[q, t], here)

    def within(r, block, k):
        return jnp.bitwise_and(match[r, block * 2 + k], 1)

    indices = pltpu.make_async_copy(match_far, match, match_sem)
    indices.start()
    for k in range(2):
        stage(k).start()
    for r in (1, 0):
        for p in range(naux):
            own_pair(r, p).start()

    barrier = pltpu.get_barrier_semaphore()
    peers = [(kpt, lax.rem(chip + d, 4) * 2 + side) for d in (1, 2, 3) for side in range(2)]
    for device in [(near, aux), (cross, aux), here] + peers:
        pl.semaphore_signal(barrier, inc=1, device_id=device, device_id_type=MESH)
    for k in range(2):
        stage(k).wait()
    indices.wait()
    index = within(0, far, core)
    for q in range(2):
        for part in range(2):
            staged[q, :, part * width : (part + 1) * width] = own_orbs[
                index, :, part * nocc + q * width : part * nocc + (q + 1) * width
            ]

    pl.semaphore_wait(barrier, 9)

    x_piece(1, 0).start()
    for q in range(2):
        for t in range(MOST):
            if (q, t) != (1, 0):
                x_piece(q, t).start()
    for r in (1, 0):
        for p in range(naux):
            given_pair(r, p).start()
    squares[...] = jnp.zeros_like(squares)

    def pass_on(q, t):
        x_piece(q, t).wait_recv()
        relay(q, t).start()
        if (q, t) == (1, 0):
            for d in (2, 1, 3):
                spread_out(1, d).start()
        else:
            share(q, t).start()

    def spread_far():
        relay(1, 0).wait_recv()
        for d in (2, 1, 3):
            spread_out(0, d).start()

    def near_quarters():
        for d in (1, 2, 3):
            spread_out(1, d).wait_recv()
        whole_share().start()

    def build(r, q):
        if r == 0:
            both = far_chunks[q][...]
        else:
            both = near_chunks[q][jnp.bitwise_xor(within(0, cross, 0), within(1, kpt, core))]
        block[0:nao, :] = both
        block[nao:, 0:width] = -both[:, width:]
        block[nao:, width:] = both[:, 0:width]

    def transform(r, q, first, last):
        def step(p):
            done = jnp.dot(held_pairs[r, p], block[...], preferred_element_type=jnp.float32).astype(jnp.bfloat16)
            real, imag = done[:, 0:width], done[:, width:]
            at = (r * combos + p) * 2 * nocc + q * 2 * width
            halves[0:nao, pl.ds(at, 2 * width)] = done
            halves[nao:, pl.ds(at, 2 * width)] = jnp.concatenate([-imag, real], axis=1)
            wide_real, wide_imag = real.astype(jnp.float32), imag.astype(jnp.float32)
            squares[...] += wide_real * wide_real + wide_imag * wide_imag

        for p in range(first, last):
            step(p)

    def pairs_of(r):
        for p in range(naux):
            own_pair(r, p).wait()
        for p in range(naux):
            given_pair(r, p).wait_recv()

    def near_here(q):
        for t in range(MOST):
            if (q, t) == (1, 0):
                whole_share().wait_recv()
            else:
                share(q, t).wait_recv()
        build(1, q)

    def far_here(q):
        for t in range(MOST):
            if (q, t) != (1, 0):
                relay(q, t).wait_recv()
        if q == 1:
            for d in (1, 2, 3):
                spread_out(0, d).wait_recv()
        build(0, q)

    pass_on(1, 0)
    pass_on(0, 0)
    pass_on(0, 1)
    spread_far()
    for t in range(2, MOST):
        pass_on(0, t)
    pairs_of(1)
    near_here(0)
    transform(1, 0, 0, 1)
    pass_on(1, 1)
    transform(1, 0, 1, 4)
    pass_on(1, 2)
    pairs_of(0)
    far_here(0)
    transform(0, 0, 0, 2)
    pass_on(1, 3)
    near_quarters()
    transform(0, 0, 2, 4)
    pass_on(1, 4)
    near_here(1)
    transform(1, 1, 0, 4)
    far_here(1)
    transform(0, 1, 0, 4)

    gain = LEVELS ** 0.5
    length = jnp.sqrt(jnp.maximum(jnp.sum(squares[...], axis=1, keepdims=True), SMALLEST))
    spread = jnp.broadcast_to(length, (nao, tile))
    scale_cols[...] = gain / spread
    for j in range(4):
        scales[:, j * tile : (j + 1) * tile] = spread[j * tile : (j + 1) * tile, :].T[0:8, :]

    def place(j):
        return pl.ds(pl.multiple_of(lax.rem(j, 4) * tile, tile), tile)

    def offset(step):
        return 2 - step + 3 * (step // 2)

    def peer(step):
        return (kpt, lax.rem(chip + offset(step), 4) * 2 + core)

    def send_scales(step):
        return remote(scales, scales_in.at[step], scale_send.at[step], scale_recv.at[step], peer(step))

    def share_scales():
        return remote(sums_scale, other_scale, share_scale_sem.at[0], share_scale_sem.at[1], here)

    for step in range(3):
        send_scales(step).start()

    def sources(owner):
        return (
            (lax.rem(owner + 1, 4), 0), (lax.rem(owner + 3, 4), 1), (lax.rem(owner + 2, 4), owner // 2),
        )

    def product(owner, j, part):
        left = halves[pl.ds(pl.multiple_of(part * nao + j * tile, tile), tile), :]
        return lax.dot_general(
            left, halves[place(owner), :], (((1,), (1,)), ((), ())), preferred_element_type=jnp.float32
        )

    below = lax.broadcasted_iota(jnp.int32, (tile, tile), 0) >= lax.broadcasted_iota(jnp.int32, (tile, tile), 1)

    def diagonal(owner):
        return jnp.where(below, product(owner, owner, 0), product(owner, owner, 1))

    def coded(value, rows_scale, cols_scale):
        return jnp.round(value * rows_scale * cols_scale).astype(jnp.int32).astype(jnp.int16)

    def send_codes(step, unit):
        return remote(
            codes.at[step, unit], codes_in.at[step, unit],
            code_send.at[step, unit], code_recv.at[step, unit], peer(step),
        )

    def send_unit(unit, step, carry):
        owner = lax.rem(chip + offset(step), 4)
        if unit == 3:
            j, value = owner, diagonal(owner)
        else:
            j, part = sources(owner)[unit]
            value = product(owner, j, part)
        codes[step, unit] = coded(value.T, scale_cols[place(owner), :], gain / scales[0:1, place(j)])
        send_codes(step, unit).start()
        return carry

    order = (2, 0, 1)
    for unit in order:
        lax.fori_loop(0, 3, functools.partial(send_unit, unit), 0)

    def own(unit):
        j, part = sources(chip)[unit]
        total[unit] = product(chip, j, part).T

    own(order[0])
    lax.fori_loop(0, 3, functools.partial(send_unit, 3), 0)

    summed = scales[...] * scales[...]
    for step in range(3):
        send_scales(step).wait()
        summed += scales_in[step] * scales_in[step]
        received = scales_in[step, 0:1, place(chip)]
        turned[step] = jnp.broadcast_to(received, (tile, tile)).T * (1.0 / LEVELS)
    sums_scale[...] = jnp.sqrt(summed)
    share_scales().start()
    own_turned = jnp.broadcast_to(sums_scale[0:1, place(chip)], (tile, tile)).T

    def gather(step, unit, j):
        send_codes(step, unit).wait()
        wide = codes_in[step, unit].astype(jnp.int32).astype(jnp.float32)
        total[unit] += wide * turned[step] * scales_in[step, 0:1, place(j)]

    def send_sum(unit, side):
        j = sources(chip)[unit][0]
        return remote(
            sums.at[unit, pl.ds(side * 64, 64)], sums_in.at[core, unit],
            sum_send.at[unit, side], sum_recv.at[core, unit], (kpt, j * 2 + side),
        )

    def take_sum(k, unit):
        return remote(
            sums.at[unit, pl.ds(0, 64)], sums_in.at[k, unit], sum_send.at[unit, 0], sum_recv.at[k, unit], here
        )

    for unit in order:
        j = sources(chip)[unit][0]
        if unit != order[0]:
            own(unit)
        for step in range(3):
            gather(step, unit, j)
        sums[unit] = coded(
            (total[unit] * (gain / own_turned) * (gain / sums_scale[0:1, place(j)])).T, 1.0, 1.0
        )
        for side in range(2):
            send_sum(unit, side).start()

    total[3] = diagonal(chip).T

    def hand(unit, part, j):
        return remote(
            handed.at[unit], out.at[core, part, :, place(j)], hand_send.at[unit], hand_recv.at[unit], here
        )

    mine = pl.ds(pl.multiple_of(core * 64, 64), 64)
    theirs = pl.ds(pl.multiple_of((1 - core) * 64, 64), 64)
    final = [(unit, part, j) for unit, (j, part) in enumerate(sources(chip))]
    final += [(3, 0, chip), (4, 1, chip)]
    for unit, part, j in final[:3]:
        handed[unit] = total[unit, theirs, :] * factor
        hand(unit, part, j).start()
        out[core, part, :, place(j)] = total[unit, mine, :] * factor
    for step in range(3):
        gather(step, 3, chip)
    packed = total[3] * factor
    turned[0] = packed.T
    strict = lax.broadcasted_iota(jnp.int32, (tile, tile), 0) > lax.broadcasted_iota(jnp.int32, (tile, tile), 1)
    real = jnp.where(strict, turned[0], packed)
    imag = jnp.where(strict, packed, 0.0)
    total[3] = real
    total[4] = imag - imag.T
    for unit, part, j in final[3:]:
        handed[unit] = total[unit, theirs, :]
        hand(unit, part, j).start()
        out[core, part, :, place(j)] = total[unit, mine, :]

    share_scales().wait()
    for same in range(2):
        k = core if same == 1 else 1 - core
        scale = sums_scale if same == 1 else other_scale
        block_rows = jnp.broadcast_to(scale[0:1, place(chip)], (tile, tile)).T * (factor / LEVELS)
        turned[same] = block_rows
        down = turned[same, mine, :]
        for unit, (j, part) in enumerate(
            ((lax.rem(chip + 3, 4), 0), (lax.rem(chip + 1, 4), 1), (lax.rem(chip + 2, 4), 1 - chip // 2))
        ):
            take_sum(k, unit).wait_recv()
            wide = sums_in[k, unit].astype(jnp.int32).astype(jnp.float32)
            sign = 1 - 2 * part
            value = wide * down * scale[0:1, place(j)]
            out[k, part, :, place(j)] = value * jnp.float32(sign) if isinstance(part, int) else value * sign.astype(jnp.float32)

    for unit in range(3):
        for side in range(2):
            send_sum(unit, side).wait_send()
    for unit, part, j in final:
        hand(unit, part, j).wait()
    for q in range(2):
        for t in range(MOST):
            x_piece(q, t).wait_send()
            relay(q, t).wait_send()
            if (q, t) != (1, 0):
                share(q, t).wait_send()
    whole_share().wait_send()
    for r in range(2):
        for d in (1, 2, 3):
            spread_out(r, d).wait_send()
        for p in range(naux):
            given_pair(r, p).wait_send()


def body(pairs, orbs, match):
    rounds, per_device, naux, nao, _ = pairs.shape
    nocc = orbs.shape[2] // 2
    factor = 1.0 / (rounds * naux * lax.axis_size("aux") * nocc) ** 0.5
    dma = pltpu.SemaphoreType.DMA
    combos = 2 * naux
    far_chunk = pltpu.VMEM((nao, nocc), jnp.bfloat16)
    near_chunk = pltpu.VMEM((per_device, nao, nocc), jnp.bfloat16)
    return pl.pallas_call(
        functools.partial(kernel, factor),
        out_shape=jax.ShapeDtypeStruct((per_device, 2, nao // 8, nao), jnp.float32),
        in_specs=[
            pl.BlockSpec(memory_space=pl.ANY),
            pl.BlockSpec(memory_space=pl.ANY),
            pl.BlockSpec(memory_space=pl.ANY),
        ],
        out_specs=pl.BlockSpec(memory_space=pltpu.VMEM),
        scratch_shapes=[
            pltpu.SMEM((2, 64), jnp.int32), dma,
            pltpu.VMEM((rounds, combos, nao, 2 * nao), jnp.bfloat16),
            pltpu.VMEM((per_device, nao, 2 * nocc), jnp.bfloat16),
            pltpu.VMEM((2, nao, nocc), jnp.bfloat16),
            far_chunk, far_chunk, near_chunk, near_chunk,
            pltpu.VMEM((2 * nao, nocc), jnp.bfloat16),
            pltpu.VMEM((2 * nao, rounds * combos * 2 * nocc), jnp.bfloat16),
            pltpu.VMEM((nao, 128), jnp.float32),
            pltpu.VMEM((nao, 128), jnp.float32),
            pltpu.VMEM((3, 4, 128, 128), jnp.int16),
            pltpu.VMEM((3, 4, 128, 128), jnp.int16),
            pltpu.VMEM((8, nao), jnp.float32),
            pltpu.VMEM((3, 8, nao), jnp.float32),
            pltpu.VMEM((8, nao), jnp.float32),
            pltpu.VMEM((8, nao), jnp.float32),
            pltpu.VMEM((3, 128, 128), jnp.float32),
            pltpu.VMEM((5, 128, 128), jnp.float32),
            pltpu.VMEM((3, 128, 128), jnp.int16),
            pltpu.VMEM((2, 3, 64, 128), jnp.int16),
            pltpu.VMEM((5, 64, 128), jnp.float32),
            dma((per_device,)), dma((rounds, naux)), dma((rounds, naux)), dma((rounds, naux)),
            dma((2, MOST)), dma((2, MOST)), dma((2, MOST)), dma((2, MOST)),
            dma((2, 3)), dma((2, 3)), dma((2, MOST)), dma((2, MOST)), dma((3, 4)), dma((3, 4)), dma((3,)), dma((3,)), dma((2,)),
            dma((3, 2)), dma((2, 3)), dma((5,)), dma((5,)),
        ],
        compiler_params=pltpu.CompilerParams(
            collective_id=0, has_side_effects=True, vmem_limit_bytes=53 << 20
        ),
    )(pairs, orbs, match)


def solution(mesh):
    placed = (P(None, "kpt", "aux", None, None), P("kpt", None, None), P())
    return jax.shard_map(
        body, mesh=mesh, in_specs=placed, out_specs=P("kpt", None, "aux", None), check_vma=False
    )
```

```python
import functools

import jax
import jax.numpy as jnp
from jax import lax
from jax.experimental import pallas as pl
from jax.experimental.pallas import tpu as pltpu
from jax.sharding import PartitionSpec as P

MESH = pl.DeviceIdType.MESH
ROUNDS = 2
LEVELS = 32000.0
SMALLEST = 1e-30
PIECES = (
    ((0, 64), (64, 64), (128, 128), (256, 128), (384, 128)),
    ((0, 32), (128, 128), (256, 128), (384, 64), (448, 64)),
)
MOST = 5


def kernel(
    factor, pairs, orbs, match_far, out,
    match, match_sem, held_pairs, own_orbs, staged, c00, c01, c10, c11, block, halves, squares, scale_cols,
    far_codes, far_in, codes, codes_in, passed_scale, joined_scale, scales, scales_in, sums_scale, other_scale, turned, total, sums, sums_in, handed,
    stage_sem, pair_sem, pair_send, pair_recv, x_send, x_recv, relay_send, relay_recv, quarter_send, quarter_recv,
    share_send, share_recv, far_send, far_recv, code_send, code_recv, scale_send, scale_recv, share_scale_sem,
    sum_send, sum_recv, hand_send, hand_recv,
):
    kpt, aux = lax.axis_index("kpt"), lax.axis_index("aux")
    chip, core = aux // 2, aux % 2
    x = kpt // 8
    rest = kpt - x * 8
    near = (x + 1 - 2 * (x % 2)) * 8 + rest
    far = (x + 2 - 4 * (x // 2)) * 8 + rest
    cross = (3 - x) * 8 + rest
    sibling = aux + 1 - 2 * core
    here = (kpt, sibling)
    nao, nocc = orbs.shape[1], orbs.shape[2] // 2
    width = nocc // 2
    naux = pairs.shape[2]
    tile = nao // 4
    combos = 2 * naux
    far_chunks, near_chunks = (c00, c01), (c10, c11)

    def remote(src, dst, send, recv, device):
        return pltpu.make_async_remote_copy(
            src_ref=src, dst_ref=dst, send_sem=send, recv_sem=recv, device_id=device, device_id_type=MESH
        )

    def own_pair(r, p):
        return pltpu.make_async_copy(
            pairs.at[r, core, p], held_pairs.at[r, core * naux + p], pair_sem.at[r, p]
        )

    def given_pair(r, p):
        return remote(
            pairs.at[r, 1 - core, p], held_pairs.at[r, core * naux + p],
            pair_send.at[r, p], pair_recv.at[r, p], here,
        )

    def stage(k):
        return pltpu.make_async_copy(orbs.at[k], own_orbs.at[k], stage_sem.at[k])

    def part_of(q, t):
        start, size = PIECES[q][t]
        if (q, t) == (1, 0):
            return pl.ds(pl.multiple_of(chip * size, size), size)
        return pl.ds(start, size)

    def spread_out(r, d):
        piece = (near_chunks[1].at[core] if r else far_chunks[1]).at[part_of(1, 0)]
        return remote(
            piece, piece, quarter_send.at[r, d - 1], quarter_recv.at[r, d - 1],
            (kpt, lax.rem(chip + d, 4) * 2 + core),
        )

    def whole_share():
        piece = near_chunks[1].at[core, pl.ds(0, 128)]
        return remote(piece, piece, share_send.at[1, 0], share_recv.at[1, 0], here)

    def x_piece(q, t):
        return remote(
            staged.at[q, part_of(q, t)], near_chunks[q].at[core, part_of(q, t)],
            x_send.at[q, t], x_recv.at[q, t], (near, aux),
        )

    def relay(q, t):
        return remote(
            near_chunks[q].at[core, part_of(q, t)], far_chunks[q].at[part_of(q, t)],
            relay_send.at[q, t], relay_recv.at[q, t], (cross, aux),
        )

    def share(q, t):
        piece = near_chunks[q].at[core, part_of(q, t)]
        return remote(piece, piece, share_send.at[q, t], share_recv.at[q, t], here)

    def within(r, block, k):
        return jnp.bitwise_and(match[r, block * 2 + k], 1)

    indices = pltpu.make_async_copy(match_far, match, match_sem)
    indices.start()
    for k in range(2):
        stage(k).start()
    for r in (1, 0):
        for p in range(naux):
            own_pair(r, p).start()

    barrier = pltpu.get_barrier_semaphore()
    peers = [(kpt, lax.rem(chip + d, 4) * 2 + side) for d in (1, 2, 3) for side in range(2)]
    for device in [(near, aux), (cross, aux), here] + peers:
        pl.semaphore_signal(barrier, inc=1, device_id=device, device_id_type=MESH)
    for k in range(2):
        stage(k).wait()
    indices.wait()
    index = within(0, far, core)
    for q in range(2):
        for part in range(2):
            staged[q, :, part * width : (part + 1) * width] = own_orbs[
                index, :, part * nocc + q * width : part * nocc + (q + 1) * width
            ]

    pl.semaphore_wait(barrier, 9)

    x_piece(1, 0).start()
    for q in range(2):
        for t in range(MOST):
            if (q, t) != (1, 0):
                x_piece(q, t).start()
    for r in (1, 0):
        for p in range(naux):
            given_pair(r, p).start()
    squares[...] = jnp.zeros_like(squares)

    def pass_on(q, t):
        x_piece(q, t).wait_recv()
        relay(q, t).start()
        if (q, t) == (1, 0):
            for d in (2, 1, 3):
                spread_out(1, d).start()
        else:
            share(q, t).start()

    def spread_far():
        relay(1, 0).wait_recv()
        for d in (2, 1, 3):
            spread_out(0, d).start()

    def near_quarters():
        for d in (1, 2, 3):
            spread_out(1, d).wait_recv()
        whole_share().start()

    def build(r, q):
        if r == 0:
            both = far_chunks[q][...]
        else:
            both = near_chunks[q][jnp.bitwise_xor(within(0, cross, 0), within(1, kpt, core))]
        block[0:nao, :] = both
        block[nao:, 0:width] = -both[:, width:]
        block[nao:, width:] = both[:, 0:width]

    def transform(r, q, first, last):
        def step(p):
            done = jnp.dot(held_pairs[r, p], block[...], preferred_element_type=jnp.float32).astype(jnp.bfloat16)
            real, imag = done[:, 0:width], done[:, width:]
            at = (r * combos + p) * 2 * nocc + q * 2 * width
            halves[0:nao, pl.ds(at, 2 * width)] = done
            halves[nao:, pl.ds(at, 2 * width)] = jnp.concatenate([-imag, real], axis=1)
            wide_real, wide_imag = real.astype(jnp.float32), imag.astype(jnp.float32)
            squares[...] += wide_real * wide_real + wide_imag * wide_imag

        for p in range(first, last):
            step(p)

    def pairs_of(r):
        for p in range(naux):
            own_pair(r, p).wait()
        for p in range(naux):
            given_pair(r, p).wait_recv()

    def near_here(q):
        for t in range(MOST):
            if (q, t) == (1, 0):
                whole_share().wait_recv()
            else:
                share(q, t).wait_recv()
        build(1, q)

    def far_here(q):
        for t in range(MOST):
            if (q, t) != (1, 0):
                relay(q, t).wait_recv()
        if q == 1:
            for d in (1, 2, 3):
                spread_out(0, d).wait_recv()
        build(0, q)

    pass_on(1, 0)
    pass_on(0, 0)
    pass_on(0, 1)
    spread_far()
    for t in range(2, MOST):
        pass_on(0, t)
    pairs_of(1)
    near_here(0)
    transform(1, 0, 0, 1)
    pass_on(1, 1)
    transform(1, 0, 1, 4)
    pass_on(1, 2)
    pairs_of(0)
    far_here(0)
    transform(0, 0, 0, 2)
    pass_on(1, 3)
    near_quarters()
    transform(0, 0, 2, 4)
    pass_on(1, 4)
    near_here(1)
    transform(1, 1, 0, 4)
    far_here(1)
    transform(0, 1, 0, 4)

    gain = LEVELS ** 0.5
    length = jnp.sqrt(jnp.maximum(jnp.sum(squares[...], axis=1, keepdims=True), SMALLEST))
    spread = jnp.broadcast_to(length, (nao, tile))
    scale_cols[...] = gain / spread
    for j in range(4):
        scales[:, j * tile : (j + 1) * tile] = spread[j * tile : (j + 1) * tile, :].T[0:8, :]

    def place(j):
        return pl.ds(pl.multiple_of(lax.rem(j, 4) * tile, tile), tile)

    def offset(step):
        return 2 - step + 3 * (step // 2)

    def peer(step):
        return (kpt, lax.rem(chip + offset(step), 4) * 2 + core)

    def send_scales(step):
        return remote(scales, scales_in.at[step], scale_send.at[step], scale_recv.at[step], peer(step))

    def share_scales():
        return remote(sums_scale, other_scale, share_scale_sem.at[0], share_scale_sem.at[1], here)

    for step in range(3):
        send_scales(step).start()

    def sources(owner):
        return (
            (lax.rem(owner + 1, 4), 0), (lax.rem(owner + 3, 4), 1), (lax.rem(owner + 2, 4), owner // 2),
        )

    def product(owner, j, part):
        left = halves[pl.ds(pl.multiple_of(part * nao + j * tile, tile), tile), :]
        return lax.dot_general(
            left, halves[place(owner), :], (((1,), (1,)), ((), ())), preferred_element_type=jnp.float32
        )

    below = lax.broadcasted_iota(jnp.int32, (tile, tile), 0) >= lax.broadcasted_iota(jnp.int32, (tile, tile), 1)

    def diagonal(owner):
        return jnp.where(below, product(owner, owner, 0), product(owner, owner, 1))

    def coded(value, rows_scale, cols_scale):
        return jnp.round(value * rows_scale * cols_scale).astype(jnp.int32).astype(jnp.int16)

    order = (2, 1, 0)
    ways = (1, 3, 1, 3)

    def chip_at(distance):
        return lax.rem(chip + distance, 4)

    def column(scale, block):
        return jnp.broadcast_to(scale[0:1, place(block)], (tile, tile)).T

    def contribution(unit, owner):
        if unit == 3:
            return owner, diagonal(owner).T
        j, part = sources(owner)[unit]
        return j, product(owner, j, part).T

    def send_far(unit):
        return remote(
            far_codes.at[unit], far_in.at[unit], far_send.at[unit], far_recv.at[unit],
            (kpt, chip_at(ways[unit]) * 2 + core),
        )

    def send_codes(joined, unit):
        distance = ways[unit] if joined else 4 - ways[unit]
        return remote(
            codes.at[joined, unit], codes_in.at[joined, unit],
            code_send.at[joined, unit], code_recv.at[joined, unit], (kpt, chip_at(distance) * 2 + core),
        )

    def coded_alone(unit, owner):
        j, value = contribution(unit, owner)
        return coded(value, scale_cols[place(owner), :], gain / scales[0:1, place(j)])

    for unit in order + (3,):
        far_codes[unit] = coded_alone(unit, chip_at(2))
        send_far(unit).start()
    for unit in order + (3,):
        codes[0, unit] = coded_alone(unit, chip_at(4 - ways[unit]))
        send_codes(0, unit).start()

    own_squares = scales[...] * scales[...]
    summed = own_squares
    for step in range(3):
        send_scales(step).wait()
        summed += scales_in[step] * scales_in[step]
    sums_scale[...] = jnp.sqrt(summed)
    share_scales().start()
    for way, step in ((0, 1), (1, 2)):
        one = scales_in[step] * scales_in[step]
        passed_scale[way] = jnp.sqrt(own_squares + one)
        joined_scale[way] = jnp.sqrt(one + scales_in[0] * scales_in[0])
        ahead = chip_at(1 + 2 * way)
        turned[way] = column(scales_in.at[step], ahead) * (1.0 / LEVELS)
        turned[2 + way] = gain / column(passed_scale.at[way], ahead)

    for unit in order + (3,):
        way = ways[unit] // 2
        j, value = contribution(unit, chip_at(ways[unit]))
        send_far(unit).wait()
        before = far_in[unit].astype(jnp.int32).astype(jnp.float32)
        value += before * turned[way] * scales_in[1 + way, 0:1, place(j)]
        codes[1, unit] = coded(value, turned[2 + way], gain / passed_scale[way, 0:1, place(j)])
        send_codes(1, unit).start()

    for way in range(2):
        turned[way] = column(scales_in.at[2 - way], chip) * (1.0 / LEVELS)
        turned[2 + way] = column(joined_scale.at[way], chip) * (1.0 / LEVELS)
    own_turned = column(sums_scale, chip)

    def gather(unit):
        way = ways[unit] // 2
        j, value = contribution(unit, chip)
        send_codes(0, unit).wait()
        wide = codes_in[0, unit].astype(jnp.int32).astype(jnp.float32)
        value += wide * turned[way] * scales_in[2 - way, 0:1, place(j)]
        send_codes(1, unit).wait()
        wide = codes_in[1, unit].astype(jnp.int32).astype(jnp.float32)
        total[unit] = value + wide * turned[2 + way] * joined_scale[way, 0:1, place(j)]

    def send_sum(unit, side):
        j = sources(chip)[unit][0]
        return remote(
            sums.at[unit, pl.ds(side * 64, 64)], sums_in.at[core, unit],
            sum_send.at[unit, side], sum_recv.at[core, unit], (kpt, j * 2 + side),
        )

    def take_sum(k, unit):
        return remote(
            sums.at[unit, pl.ds(0, 64)], sums_in.at[k, unit], sum_send.at[unit, 0], sum_recv.at[k, unit], here
        )

    for unit in order:
        j = sources(chip)[unit][0]
        gather(unit)
        sums[unit] = coded(
            (total[unit] * (gain / own_turned) * (gain / sums_scale[0:1, place(j)])).T, 1.0, 1.0
        )
        for side in range(2):
            send_sum(unit, side).start()

    def hand(unit, part, j):
        return remote(
            handed.at[unit], out.at[core, part, :, place(j)], hand_send.at[unit], hand_recv.at[unit], here
        )

    mine = pl.ds(pl.multiple_of(core * 64, 64), 64)
    theirs = pl.ds(pl.multiple_of((1 - core) * 64, 64), 64)
    final = [(unit, part, j) for unit, (j, part) in enumerate(sources(chip))]
    final += [(3, 0, chip), (4, 1, chip)]
    for unit, part, j in final[:3]:
        handed[unit] = total[unit, theirs, :] * factor
        hand(unit, part, j).start()
        out[core, part, :, place(j)] = total[unit, mine, :] * factor
    gather(3)
    packed = total[3] * factor
    turned[0] = packed.T
    strict = lax.broadcasted_iota(jnp.int32, (tile, tile), 0) > lax.broadcasted_iota(jnp.int32, (tile, tile), 1)
    real = jnp.where(strict, turned[0], packed)
    imag = jnp.where(strict, packed, 0.0)
    total[3] = real
    total[4] = imag - imag.T
    for unit, part, j in final[3:]:
        handed[unit] = total[unit, theirs, :]
        hand(unit, part, j).start()
        out[core, part, :, place(j)] = total[unit, mine, :]

    share_scales().wait()
    for same in range(2):
        k = core if same == 1 else 1 - core
        scale = sums_scale if same == 1 else other_scale
        block_rows = jnp.broadcast_to(scale[0:1, place(chip)], (tile, tile)).T * (factor / LEVELS)
        turned[same] = block_rows
        down = turned[same, mine, :]
        for unit, (j, part) in enumerate(
            ((lax.rem(chip + 3, 4), 0), (lax.rem(chip + 1, 4), 1), (lax.rem(chip + 2, 4), 1 - chip // 2))
        ):
            take_sum(k, unit).wait_recv()
            wide = sums_in[k, unit].astype(jnp.int32).astype(jnp.float32)
            sign = 1 - 2 * part
            value = wide * down * scale[0:1, place(j)]
            out[k, part, :, place(j)] = value * jnp.float32(sign) if isinstance(part, int) else value * sign.astype(jnp.float32)

    for unit in range(3):
        for side in range(2):
            send_sum(unit, side).wait_send()
    for unit, part, j in final:
        hand(unit, part, j).wait()
    for q in range(2):
        for t in range(MOST):
            x_piece(q, t).wait_send()
            relay(q, t).wait_send()
            if (q, t) != (1, 0):
                share(q, t).wait_send()
    whole_share().wait_send()
    for r in range(2):
        for d in (1, 2, 3):
            spread_out(r, d).wait_send()
        for p in range(naux):
            given_pair(r, p).wait_send()


def body(pairs, orbs, match):
    rounds, per_device, naux, nao, _ = pairs.shape
    nocc = orbs.shape[2] // 2
    factor = 1.0 / (rounds * naux * lax.axis_size("aux") * nocc) ** 0.5
    dma = pltpu.SemaphoreType.DMA
    combos = 2 * naux
    far_chunk = pltpu.VMEM((nao, nocc), jnp.bfloat16)
    near_chunk = pltpu.VMEM((per_device, nao, nocc), jnp.bfloat16)
    return pl.pallas_call(
        functools.partial(kernel, factor),
        out_shape=jax.ShapeDtypeStruct((per_device, 2, nao // 8, nao), jnp.float32),
        in_specs=[
            pl.BlockSpec(memory_space=pl.ANY),
            pl.BlockSpec(memory_space=pl.ANY),
            pl.BlockSpec(memory_space=pl.ANY),
        ],
        out_specs=pl.BlockSpec(memory_space=pltpu.VMEM),
        scratch_shapes=[
            pltpu.SMEM((2, 64), jnp.int32), dma,
            pltpu.VMEM((rounds, combos, nao, 2 * nao), jnp.bfloat16),
            pltpu.VMEM((per_device, nao, 2 * nocc), jnp.bfloat16),
            pltpu.VMEM((2, nao, nocc), jnp.bfloat16),
            far_chunk, far_chunk, near_chunk, near_chunk,
            pltpu.VMEM((2 * nao, nocc), jnp.bfloat16),
            pltpu.VMEM((2 * nao, rounds * combos * 2 * nocc), jnp.bfloat16),
            pltpu.VMEM((nao, 128), jnp.float32),
            pltpu.VMEM((nao, 128), jnp.float32),
            pltpu.VMEM((4, 128, 128), jnp.int16),
            pltpu.VMEM((4, 128, 128), jnp.int16),
            pltpu.VMEM((2, 4, 128, 128), jnp.int16),
            pltpu.VMEM((2, 4, 128, 128), jnp.int16),
            pltpu.VMEM((2, 8, nao), jnp.float32),
            pltpu.VMEM((2, 8, nao), jnp.float32),
            pltpu.VMEM((8, nao), jnp.float32),
            pltpu.VMEM((3, 8, nao), jnp.float32),
            pltpu.VMEM((8, nao), jnp.float32),
            pltpu.VMEM((8, nao), jnp.float32),
            pltpu.VMEM((4, 128, 128), jnp.float32),
            pltpu.VMEM((5, 128, 128), jnp.float32),
            pltpu.VMEM((3, 128, 128), jnp.int16),
            pltpu.VMEM((2, 3, 64, 128), jnp.int16),
            pltpu.VMEM((5, 64, 128), jnp.float32),
            dma((per_device,)), dma((rounds, naux)), dma((rounds, naux)), dma((rounds, naux)),
            dma((2, MOST)), dma((2, MOST)), dma((2, MOST)), dma((2, MOST)),
            dma((2, 3)), dma((2, 3)), dma((2, MOST)), dma((2, MOST)), dma((4,)), dma((4,)), dma((2, 4)), dma((2, 4)), dma((3,)), dma((3,)), dma((2,)),
            dma((3, 2)), dma((2, 3)), dma((5,)), dma((5,)),
        ],
        compiler_params=pltpu.CompilerParams(
            collective_id=0, has_side_effects=True, vmem_limit_bytes=53 << 20
        ),
    )(pairs, orbs, match)


def solution(mesh):
    placed = (P(None, "kpt", "aux", None, None), P("kpt", None, None), P())
    return jax.shard_map(
        body, mesh=mesh, in_specs=placed, out_specs=P("kpt", None, "aux", None), check_vma=False
    )
```

```python
import functools

import jax
import jax.numpy as jnp
from jax import lax
from jax.experimental import pallas as pl
from jax.experimental.pallas import tpu as pltpu
from jax.sharding import PartitionSpec as P

MESH = pl.DeviceIdType.MESH
ROUNDS = 2
LEVELS = 32000.0
SMALLEST = 1e-30
PIECES = (
    ((0, 64), (64, 64), (128, 128), (256, 128), (384, 128)),
    ((0, 32), (128, 128), (256, 128), (384, 64), (448, 64)),
)
MOST = 5


def kernel(
    factor, pairs, orbs, match_far, out,
    match, match_sem, held_pairs, own_orbs, staged, c00, c01, c10, c11, block, halves, squares, scale_cols,
    far_codes, far_in, codes, codes_in, passed_scale, joined_scale, scales, scales_in, sums_scale, other_scale, turned, total, sums, sums_in, handed,
    stage_sem, pair_sem, pair_send, pair_recv, x_send, x_recv, relay_send, relay_recv, quarter_send, quarter_recv,
    share_send, share_recv, far_send, far_recv, code_send, code_recv, scale_send, scale_recv, share_scale_sem,
    sum_send, sum_recv, hand_send, hand_recv,
):
    kpt, aux = lax.axis_index("kpt"), lax.axis_index("aux")
    chip, core = aux // 2, aux % 2
    x = kpt // 8
    rest = kpt - x * 8
    near = (x + 1 - 2 * (x % 2)) * 8 + rest
    far = (x + 2 - 4 * (x // 2)) * 8 + rest
    cross = (3 - x) * 8 + rest
    sibling = aux + 1 - 2 * core
    here = (kpt, sibling)
    nao, nocc = orbs.shape[1], orbs.shape[2] // 2
    width = nocc // 2
    naux = pairs.shape[2]
    tile = nao // 4
    combos = 2 * naux
    far_chunks, near_chunks = (c00, c01), (c10, c11)

    def remote(src, dst, send, recv, device):
        return pltpu.make_async_remote_copy(
            src_ref=src, dst_ref=dst, send_sem=send, recv_sem=recv, device_id=device, device_id_type=MESH
        )

    def own_pair(r, p):
        return pltpu.make_async_copy(
            pairs.at[r, core, p], held_pairs.at[r, core * naux + p], pair_sem.at[r, p]
        )

    def given_pair(r, p):
        return remote(
            pairs.at[r, 1 - core, p], held_pairs.at[r, core * naux + p],
            pair_send.at[r, p], pair_recv.at[r, p], here,
        )

    def stage(k):
        return pltpu.make_async_copy(orbs.at[k], own_orbs.at[k], stage_sem.at[k])

    def part_of(q, t):
        start, size = PIECES[q][t]
        if (q, t) == (1, 0):
            return pl.ds(pl.multiple_of(chip * size, size), size)
        return pl.ds(start, size)

    def spread_out(r, d):
        piece = (near_chunks[1].at[core] if r else far_chunks[1]).at[part_of(1, 0)]
        return remote(
            piece, piece, quarter_send.at[r, d - 1], quarter_recv.at[r, d - 1],
            (kpt, lax.rem(chip + d, 4) * 2 + core),
        )

    def whole_share():
        piece = near_chunks[1].at[core, pl.ds(0, 128)]
        return remote(piece, piece, share_send.at[1, 0], share_recv.at[1, 0], here)

    def x_piece(q, t):
        return remote(
            staged.at[q, part_of(q, t)], near_chunks[q].at[core, part_of(q, t)],
            x_send.at[q, t], x_recv.at[q, t], (near, aux),
        )

    def relay(q, t):
        return remote(
            near_chunks[q].at[core, part_of(q, t)], far_chunks[q].at[part_of(q, t)],
            relay_send.at[q, t], relay_recv.at[q, t], (cross, aux),
        )

    def share(q, t):
        piece = near_chunks[q].at[core, part_of(q, t)]
        return remote(piece, piece, share_send.at[q, t], share_recv.at[q, t], here)

    def within(r, block, k):
        return jnp.bitwise_and(match[r, block * 2 + k], 1)

    indices = pltpu.make_async_copy(match_far, match, match_sem)
    indices.start()
    for k in range(2):
        stage(k).start()
    for r in (1, 0):
        for p in range(naux):
            own_pair(r, p).start()

    barrier = pltpu.get_barrier_semaphore()
    peers = [(kpt, lax.rem(chip + d, 4) * 2 + side) for d in (1, 2, 3) for side in range(2)]
    for device in [(near, aux), (cross, aux), here] + peers:
        pl.semaphore_signal(barrier, inc=1, device_id=device, device_id_type=MESH)
    for k in range(2):
        stage(k).wait()
    indices.wait()
    index = within(0, far, core)
    for q in range(2):
        for part in range(2):
            staged[q, :, part * width : (part + 1) * width] = own_orbs[
                index, :, part * nocc + q * width : part * nocc + (q + 1) * width
            ]

    pl.semaphore_wait(barrier, 9)

    x_piece(1, 0).start()
    for q in range(2):
        for t in range(MOST):
            if (q, t) != (1, 0):
                x_piece(q, t).start()
    for r in (1, 0):
        for p in range(naux):
            given_pair(r, p).start()
    squares[...] = jnp.zeros_like(squares)

    def pass_on(q, t):
        x_piece(q, t).wait_recv()
        relay(q, t).start()
        if (q, t) == (1, 0):
            for d in (2, 1, 3):
                spread_out(1, d).start()
        else:
            share(q, t).start()

    def spread_far():
        relay(1, 0).wait_recv()
        for d in (2, 1, 3):
            spread_out(0, d).start()

    def near_quarters():
        for d in (1, 2, 3):
            spread_out(1, d).wait_recv()
        whole_share().start()

    def build(r, q):
        if r == 0:
            both = far_chunks[q][...]
        else:
            both = near_chunks[q][jnp.bitwise_xor(within(0, cross, 0), within(1, kpt, core))]
        block[0:nao, :] = both
        block[nao:, 0:width] = -both[:, width:]
        block[nao:, width:] = both[:, 0:width]

    def transform(r, q, first, last):
        def step(p):
            done = jnp.dot(held_pairs[r, p], block[...], preferred_element_type=jnp.float32).astype(jnp.bfloat16)
            real, imag = done[:, 0:width], done[:, width:]
            at = (r * combos + p) * 2 * nocc + q * 2 * width
            halves[0:nao, pl.ds(at, 2 * width)] = done
            halves[nao:, pl.ds(at, 2 * width)] = jnp.concatenate([-imag, real], axis=1)
            wide_real, wide_imag = real.astype(jnp.float32), imag.astype(jnp.float32)
            squares[...] += wide_real * wide_real + wide_imag * wide_imag

        for p in range(first, last):
            step(p)

    def pairs_of(r):
        for p in range(naux):
            own_pair(r, p).wait()
        for p in range(naux):
            given_pair(r, p).wait_recv()

    def near_here(q):
        for t in range(MOST):
            if (q, t) == (1, 0):
                whole_share().wait_recv()
            else:
                share(q, t).wait_recv()
        build(1, q)

    def far_here(q):
        for t in range(MOST):
            if (q, t) != (1, 0):
                relay(q, t).wait_recv()
        if q == 1:
            for d in (1, 2, 3):
                spread_out(0, d).wait_recv()
        build(0, q)

    pass_on(1, 0)
    pass_on(0, 0)
    pass_on(0, 1)
    spread_far()
    for t in range(2, MOST):
        pass_on(0, t)
    pairs_of(1)
    near_here(0)
    transform(1, 0, 0, 1)
    pass_on(1, 1)
    transform(1, 0, 1, 4)
    pass_on(1, 2)
    pairs_of(0)
    far_here(0)
    transform(0, 0, 0, 2)
    pass_on(1, 3)
    near_quarters()
    transform(0, 0, 2, 4)
    pass_on(1, 4)
    near_here(1)
    transform(1, 1, 0, 4)
    far_here(1)
    transform(0, 1, 0, 4)

    gain = LEVELS ** 0.5
    length = jnp.sqrt(jnp.maximum(jnp.sum(squares[...], axis=1, keepdims=True), SMALLEST))
    spread = jnp.broadcast_to(length, (nao, tile))
    scale_cols[...] = gain / spread
    for j in range(4):
        scales[:, j * tile : (j + 1) * tile] = spread[j * tile : (j + 1) * tile, :].T[0:8, :]

    def place(j):
        return pl.ds(pl.multiple_of(lax.rem(j, 4) * tile, tile), tile)

    def offset(step):
        return 2 - step + 3 * (step // 2)

    def peer(step):
        return (kpt, lax.rem(chip + offset(step), 4) * 2 + core)

    def send_scales(step):
        return remote(scales, scales_in.at[step], scale_send.at[step], scale_recv.at[step], peer(step))

    def share_scales():
        return remote(sums_scale, other_scale, share_scale_sem.at[0], share_scale_sem.at[1], here)

    for step in range(3):
        send_scales(step).start()

    def sources(owner):
        return (
            (lax.rem(owner + 1, 4), 0), (lax.rem(owner + 3, 4), 1), (lax.rem(owner + 2, 4), owner // 2),
        )

    def product(owner, j, part):
        left = halves[pl.ds(pl.multiple_of(part * nao + j * tile, tile), tile), :]
        return lax.dot_general(
            left, halves[place(owner), :], (((1,), (1,)), ((), ())), preferred_element_type=jnp.float32
        )

    below = lax.broadcasted_iota(jnp.int32, (tile, tile), 0) >= lax.broadcasted_iota(jnp.int32, (tile, tile), 1)

    def diagonal(owner):
        return jnp.where(below, product(owner, owner, 0), product(owner, owner, 1))

    def coded(value, rows_scale, cols_scale):
        return jnp.round(value * rows_scale * cols_scale).astype(jnp.int32).astype(jnp.int16)

    order = (2, 1, 0)
    ways = (1, 3, 1, 3)

    def chip_at(distance):
        return lax.rem(chip + distance, 4)

    def column(scale, block):
        return jnp.broadcast_to(scale[0:1, place(block)], (tile, tile)).T

    def contribution(unit, owner):
        if unit == 3:
            return owner, diagonal(owner).T
        j, part = sources(owner)[unit]
        return j, product(owner, j, part).T

    def send_far(unit):
        return remote(
            far_codes.at[unit], far_in.at[unit], far_send.at[unit], far_recv.at[unit],
            (kpt, chip_at(ways[unit]) * 2 + core),
        )

    def send_codes(joined, unit):
        distance = ways[unit] if joined else 4 - ways[unit]
        return remote(
            codes.at[joined, unit], codes_in.at[joined, unit],
            code_send.at[joined, unit], code_recv.at[joined, unit], (kpt, chip_at(distance) * 2 + core),
        )

    def coded_alone(unit, owner):
        j, value = contribution(unit, owner)
        return coded(value, scale_cols[place(owner), :], gain / scales[0:1, place(j)])

    for unit in order + (3,):
        far_codes[unit] = coded_alone(unit, chip_at(2))
        send_far(unit).start()
    for unit in order + (3,):
        codes[0, unit] = coded_alone(unit, chip_at(4 - ways[unit]))
        send_codes(0, unit).start()

    own_squares = scales[...] * scales[...]
    summed = own_squares
    for step in range(3):
        send_scales(step).wait()
        summed += scales_in[step] * scales_in[step]
    sums_scale[...] = jnp.sqrt(summed)
    share_scales().start()
    for way, step in ((0, 1), (1, 2)):
        one = scales_in[step] * scales_in[step]
        passed_scale[way] = jnp.sqrt(own_squares + one)
        joined_scale[way] = jnp.sqrt(one + scales_in[0] * scales_in[0])
        ahead = chip_at(1 + 2 * way)
        turned[way] = column(scales_in.at[step], ahead) * (1.0 / LEVELS)
        turned[2 + way] = gain / column(passed_scale.at[way], ahead)

    for unit in order + (3,):
        way = ways[unit] // 2
        j, value = contribution(unit, chip_at(ways[unit]))
        send_far(unit).wait()
        before = far_in[unit].astype(jnp.int32).astype(jnp.float32)
        value += before * turned[way] * scales_in[1 + way, 0:1, place(j)]
        codes[1, unit] = coded(value, turned[2 + way], gain / passed_scale[way, 0:1, place(j)])
        send_codes(1, unit).start()

    for way in range(2):
        turned[way] = column(scales_in.at[2 - way], chip) * (1.0 / LEVELS)
        turned[2 + way] = column(joined_scale.at[way], chip) * (1.0 / LEVELS)
    own_turned = column(sums_scale, chip)

    def gather(unit):
        way = ways[unit] // 2
        j, value = contribution(unit, chip)
        send_codes(0, unit).wait()
        wide = codes_in[0, unit].astype(jnp.int32).astype(jnp.float32)
        value += wide * turned[way] * scales_in[2 - way, 0:1, place(j)]
        send_codes(1, unit).wait()
        wide = codes_in[1, unit].astype(jnp.int32).astype(jnp.float32)
        total[unit] = value + wide * turned[2 + way] * joined_scale[way, 0:1, place(j)]

    def send_sum(unit, side):
        j = sources(chip)[unit][0]
        return remote(
            sums.at[unit, pl.ds(side * 64, 64)], sums_in.at[core, unit],
            sum_send.at[unit, side], sum_recv.at[core, unit], (kpt, j * 2 + side),
        )

    def take_sum(k, unit):
        return remote(
            sums.at[unit, pl.ds(0, 64)], sums_in.at[k, unit], sum_send.at[unit, 0], sum_recv.at[k, unit], here
        )

    for unit in order:
        j = sources(chip)[unit][0]
        gather(unit)
        sums[unit] = coded(
            (total[unit] * (gain / own_turned) * (gain / sums_scale[0:1, place(j)])).T, 1.0, 1.0
        )
        for side in range(2):
            send_sum(unit, side).start()

    def hand(unit, part, j):
        return remote(
            handed.at[unit], out.at[core, part, :, place(j)], hand_send.at[unit], hand_recv.at[unit], here
        )

    mine = pl.ds(pl.multiple_of(core * 64, 64), 64)
    theirs = pl.ds(pl.multiple_of((1 - core) * 64, 64), 64)
    final = [(unit, part, j) for unit, (j, part) in enumerate(sources(chip))]
    final += [(3, 0, chip), (4, 1, chip)]
    for unit, part, j in final[:3]:
        handed[unit] = total[unit, theirs, :] * factor
        hand(unit, part, j).start()
        out[core, part, :, place(j)] = total[unit, mine, :] * factor
    gather(3)
    packed = total[3] * factor
    turned[0] = packed.T
    strict = lax.broadcasted_iota(jnp.int32, (tile, tile), 0) > lax.broadcasted_iota(jnp.int32, (tile, tile), 1)
    real = jnp.where(strict, turned[0], packed)
    imag = jnp.where(strict, packed, 0.0)
    total[3] = real
    total[4] = imag - imag.T
    for unit, part, j in final[3:]:
        handed[unit] = total[unit, theirs, :]
        hand(unit, part, j).start()
        out[core, part, :, place(j)] = total[unit, mine, :]

    share_scales().wait()
    for same in range(2):
        k = core if same == 1 else 1 - core
        scale = sums_scale if same == 1 else other_scale
        block_rows = jnp.broadcast_to(scale[0:1, place(chip)], (tile, tile)).T * (factor / LEVELS)
        turned[same] = block_rows
        down = turned[same, mine, :]
        for unit, (j, part) in enumerate(
            ((lax.rem(chip + 3, 4), 0), (lax.rem(chip + 1, 4), 1), (lax.rem(chip + 2, 4), 1 - chip // 2))
        ):
            take_sum(k, unit).wait_recv()
            wide = sums_in[k, unit].astype(jnp.int32).astype(jnp.float32)
            sign = 1 - 2 * part
            value = wide * down * scale[0:1, place(j)]
            out[k, part, :, place(j)] = value * jnp.float32(sign) if isinstance(part, int) else value * sign.astype(jnp.float32)

    for unit in range(3):
        for side in range(2):
            send_sum(unit, side).wait_send()
    for unit, part, j in final:
        hand(unit, part, j).wait()
    for q in range(2):
        for t in range(MOST):
            x_piece(q, t).wait_send()
            relay(q, t).wait_send()
            if (q, t) != (1, 0):
                share(q, t).wait_send()
    whole_share().wait_send()
    for r in range(2):
        for d in (1, 2, 3):
            spread_out(r, d).wait_send()
        for p in range(naux):
            given_pair(r, p).wait_send()


def body(pairs, orbs, match):
    rounds, per_device, naux, nao, _ = pairs.shape
    nocc = orbs.shape[2] // 2
    factor = 1.0 / (rounds * naux * lax.axis_size("aux") * nocc) ** 0.5
    dma = pltpu.SemaphoreType.DMA
    combos = 2 * naux
    far_chunk = pltpu.VMEM((nao, nocc), jnp.bfloat16)
    near_chunk = pltpu.VMEM((per_device, nao, nocc), jnp.bfloat16)
    return pl.pallas_call(
        functools.partial(kernel, factor),
        out_shape=jax.ShapeDtypeStruct((per_device, 2, nao // 8, nao), jnp.float32),
        in_specs=[
            pl.BlockSpec(memory_space=pl.ANY),
            pl.BlockSpec(memory_space=pl.ANY),
            pl.BlockSpec(memory_space=pl.ANY),
        ],
        out_specs=pl.BlockSpec(memory_space=pltpu.VMEM),
        scratch_shapes=[
            pltpu.SMEM((2, 64), jnp.int32), dma,
            pltpu.VMEM((rounds, combos, nao, 2 * nao), jnp.bfloat16),
            pltpu.VMEM((per_device, nao, 2 * nocc), jnp.bfloat16),
            pltpu.VMEM((2, nao, nocc), jnp.bfloat16),
            far_chunk, far_chunk, near_chunk, near_chunk,
            pltpu.VMEM((2 * nao, nocc), jnp.bfloat16),
            pltpu.VMEM((2 * nao, rounds * combos * 2 * nocc), jnp.bfloat16),
            pltpu.VMEM((nao, 128), jnp.float32),
            pltpu.VMEM((nao, 128), jnp.float32),
            pltpu.VMEM((4, 128, 128), jnp.int16),
            pltpu.VMEM((4, 128, 128), jnp.int16),
            pltpu.VMEM((2, 4, 128, 128), jnp.int16),
            pltpu.VMEM((2, 4, 128, 128), jnp.int16),
            pltpu.VMEM((2, 8, nao), jnp.float32),
            pltpu.VMEM((2, 8, nao), jnp.float32),
            pltpu.VMEM((8, nao), jnp.float32),
            pltpu.VMEM((3, 8, nao), jnp.float32),
            pltpu.VMEM((8, nao), jnp.float32),
            pltpu.VMEM((8, nao), jnp.float32),
            pltpu.VMEM((4, 128, 128), jnp.float32),
            pltpu.VMEM((5, 128, 128), jnp.float32),
            pltpu.VMEM((3, 128, 128), jnp.int16),
            pltpu.VMEM((2, 3, 64, 128), jnp.int16),
            pltpu.VMEM((5, 64, 128), jnp.float32),
            dma((per_device,)), dma((rounds, naux)), dma((rounds, naux)), dma((rounds, naux)),
            dma((2, MOST)), dma((2, MOST)), dma((2, MOST)), dma((2, MOST)),
            dma((2, 3)), dma((2, 3)), dma((2, MOST)), dma((2, MOST)), dma((4,)), dma((4,)), dma((2, 4)), dma((2, 4)), dma((3,)), dma((3,)), dma((2,)),
            dma((3, 2)), dma((2, 3)), dma((5,)), dma((5,)),
        ],
        compiler_params=pltpu.CompilerParams(
            collective_id=0, has_side_effects=True, vmem_limit_bytes=53 << 20
        ),
    )(pairs, orbs, pltpu.with_memory_space_constraint(match, pltpu.HBM))


def solution(mesh):
    placed = (P(None, "kpt", "aux", None, None), P("kpt", None, None), P())
    return jax.shard_map(
        body, mesh=mesh, in_specs=placed, out_specs=P("kpt", None, "aux", None), check_vma=False
    )
```

```python
import functools

import jax
import jax.numpy as jnp
from jax import lax
from jax.experimental import pallas as pl
from jax.experimental.pallas import tpu as pltpu
from jax.sharding import PartitionSpec as P

MESH = pl.DeviceIdType.MESH
ROUNDS = 2
LEVELS = 32000.0
SMALLEST = 1e-30
PIECES = (
    ((0, 64), (64, 64), (128, 128), (256, 128), (384, 128)),
    ((0, 32), (128, 128), (256, 128), (384, 64), (448, 64)),
)
MOST = 5


def kernel(
    factor, pairs, orbs, match_far, out,
    match, match_sem, held_pairs, own_orbs, staged, c00, c01, c10, c11, block, halves, squares, scale_cols,
    far_codes, far_in, codes, codes_in, passed_scale, joined_scale, scales, scales_in, sums_scale, other_scale, turned, total, sums, sums_in, handed,
    stage_sem, pair_sem, pair_send, pair_recv, x_send, x_recv, relay_send, relay_recv, quarter_send, quarter_recv,
    share_send, share_recv, far_send, far_recv, code_send, code_recv, scale_send, scale_recv, share_scale_sem,
    sum_send, sum_recv, hand_send, hand_recv,
):
    kpt, aux = lax.axis_index("kpt"), lax.axis_index("aux")
    chip, core = aux // 2, aux % 2
    x = kpt // 8
    rest = kpt - x * 8
    near = (x + 1 - 2 * (x % 2)) * 8 + rest
    far = (x + 2 - 4 * (x // 2)) * 8 + rest
    cross = (3 - x) * 8 + rest
    sibling = aux + 1 - 2 * core
    here = (kpt, sibling)
    nao, nocc = orbs.shape[1], orbs.shape[2] // 2
    width = nocc // 2
    naux = pairs.shape[2]
    tile = nao // 4
    combos = 2 * naux
    far_chunks, near_chunks = (c00, c01), (c10, c11)

    def remote(src, dst, send, recv, device):
        return pltpu.make_async_remote_copy(
            src_ref=src, dst_ref=dst, send_sem=send, recv_sem=recv, device_id=device, device_id_type=MESH
        )

    def own_pair(r, p):
        return pltpu.make_async_copy(
            pairs.at[r, core, p], held_pairs.at[r, core * naux + p], pair_sem.at[r, p]
        )

    def given_pair(r, p):
        return remote(
            pairs.at[r, 1 - core, p], held_pairs.at[r, core * naux + p],
            pair_send.at[r, p], pair_recv.at[r, p], here,
        )

    def stage(k):
        return pltpu.make_async_copy(orbs.at[k], own_orbs.at[k], stage_sem.at[k])

    def part_of(q, t):
        start, size = PIECES[q][t]
        if (q, t) == (1, 0):
            return pl.ds(pl.multiple_of(chip * size, size), size)
        return pl.ds(start, size)

    def spread_out(r, d):
        piece = (near_chunks[1].at[core] if r else far_chunks[1]).at[part_of(1, 0)]
        return remote(
            piece, piece, quarter_send.at[r, d - 1], quarter_recv.at[r, d - 1],
            (kpt, lax.rem(chip + d, 4) * 2 + core),
        )

    def whole_share():
        piece = near_chunks[1].at[core, pl.ds(0, 128)]
        return remote(piece, piece, share_send.at[1, 0], share_recv.at[1, 0], here)

    def x_piece(q, t):
        return remote(
            staged.at[q, part_of(q, t)], near_chunks[q].at[core, part_of(q, t)],
            x_send.at[q, t], x_recv.at[q, t], (near, aux),
        )

    def relay(q, t):
        return remote(
            near_chunks[q].at[core, part_of(q, t)], far_chunks[q].at[part_of(q, t)],
            relay_send.at[q, t], relay_recv.at[q, t], (cross, aux),
        )

    def share(q, t):
        piece = near_chunks[q].at[core, part_of(q, t)]
        return remote(piece, piece, share_send.at[q, t], share_recv.at[q, t], here)

    def within(r, block, k):
        return jnp.bitwise_and(match[r, block * 2 + k], 1)

    barrier = pltpu.get_barrier_semaphore()
    peers = [(kpt, lax.rem(chip + d, 4) * 2 + side) for d in (1, 2, 3) for side in range(2)]
    for device in [(near, aux), (cross, aux), here] + peers:
        pl.semaphore_signal(barrier, inc=1, device_id=device, device_id_type=MESH)
    indices = pltpu.make_async_copy(match_far, match, match_sem)
    indices.start()
    for k in range(2):
        stage(k).start()
    for k in range(2):
        stage(k).wait()
    indices.wait()
    index = within(0, far, core)
    for q in range(2):
        for part in range(2):
            staged[q, :, part * width : (part + 1) * width] = own_orbs[
                index, :, part * nocc + q * width : part * nocc + (q + 1) * width
            ]

    pl.semaphore_wait(barrier, 9)

    x_piece(1, 0).start()
    for q in range(2):
        for t in range(MOST):
            if (q, t) != (1, 0):
                x_piece(q, t).start()
    for r in (1, 0):
        for p in range(naux):
            own_pair(r, p).start()
            given_pair(r, p).start()
    squares[...] = jnp.zeros_like(squares)

    def pass_on(q, t):
        x_piece(q, t).wait_recv()
        relay(q, t).start()
        if (q, t) == (1, 0):
            for d in (2, 1, 3):
                spread_out(1, d).start()
        else:
            share(q, t).start()

    def spread_far():
        relay(1, 0).wait_recv()
        for d in (2, 1, 3):
            spread_out(0, d).start()

    def near_quarters():
        for d in (1, 2, 3):
            spread_out(1, d).wait_recv()
        whole_share().start()

    def build(r, q):
        if r == 0:
            both = far_chunks[q][...]
        else:
            both = near_chunks[q][jnp.bitwise_xor(within(0, cross, 0), within(1, kpt, core))]
        block[0:nao, :] = both
        block[nao:, 0:width] = -both[:, width:]
        block[nao:, width:] = both[:, 0:width]

    def transform(r, q, first, last):
        def step(p):
            done = jnp.dot(held_pairs[r, p], block[...], preferred_element_type=jnp.float32).astype(jnp.bfloat16)
            real, imag = done[:, 0:width], done[:, width:]
            at = (r * combos + p) * 2 * nocc + q * 2 * width
            halves[0:nao, pl.ds(at, 2 * width)] = done
            halves[nao:, pl.ds(at, 2 * width)] = jnp.concatenate([-imag, real], axis=1)
            wide_real, wide_imag = real.astype(jnp.float32), imag.astype(jnp.float32)
            squares[...] += wide_real * wide_real + wide_imag * wide_imag

        for p in range(first, last):
            step(p)

    def pairs_of(r):
        for p in range(naux):
            own_pair(r, p).wait()
        for p in range(naux):
            given_pair(r, p).wait_recv()

    def near_here(q):
        for t in range(MOST):
            if (q, t) == (1, 0):
                whole_share().wait_recv()
            else:
                share(q, t).wait_recv()
        build(1, q)

    def far_here(q):
        for t in range(MOST):
            if (q, t) != (1, 0):
                relay(q, t).wait_recv()
        if q == 1:
            for d in (1, 2, 3):
                spread_out(0, d).wait_recv()
        build(0, q)

    pass_on(1, 0)
    pass_on(0, 0)
    pass_on(0, 1)
    spread_far()
    for t in range(2, MOST):
        pass_on(0, t)
    pairs_of(1)
    near_here(0)
    transform(1, 0, 0, 1)
    pass_on(1, 1)
    transform(1, 0, 1, 4)
    pass_on(1, 2)
    pairs_of(0)
    far_here(0)
    transform(0, 0, 0, 2)
    pass_on(1, 3)
    near_quarters()
    transform(0, 0, 2, 4)
    pass_on(1, 4)
    near_here(1)
    transform(1, 1, 0, 4)
    far_here(1)
    transform(0, 1, 0, 4)

    gain = LEVELS ** 0.5
    length = jnp.sqrt(jnp.maximum(jnp.sum(squares[...], axis=1, keepdims=True), SMALLEST))
    spread = jnp.broadcast_to(length, (nao, tile))
    scale_cols[...] = gain / spread
    for j in range(4):
        scales[:, j * tile : (j + 1) * tile] = spread[j * tile : (j + 1) * tile, :].T[0:8, :]

    def place(j):
        return pl.ds(pl.multiple_of(lax.rem(j, 4) * tile, tile), tile)

    def offset(step):
        return 2 - step + 3 * (step // 2)

    def peer(step):
        return (kpt, lax.rem(chip + offset(step), 4) * 2 + core)

    def send_scales(step):
        return remote(scales, scales_in.at[step], scale_send.at[step], scale_recv.at[step], peer(step))

    def share_scales():
        return remote(sums_scale, other_scale, share_scale_sem.at[0], share_scale_sem.at[1], here)

    for step in range(3):
        send_scales(step).start()

    def sources(owner):
        return (
            (lax.rem(owner + 1, 4), 0), (lax.rem(owner + 3, 4), 1), (lax.rem(owner + 2, 4), owner // 2),
        )

    def product(owner, j, part):
        left = halves[pl.ds(pl.multiple_of(part * nao + j * tile, tile), tile), :]
        return lax.dot_general(
            left, halves[place(owner), :], (((1,), (1,)), ((), ())), preferred_element_type=jnp.float32
        )

    below = lax.broadcasted_iota(jnp.int32, (tile, tile), 0) >= lax.broadcasted_iota(jnp.int32, (tile, tile), 1)

    def diagonal(owner):
        return jnp.where(below, product(owner, owner, 0), product(owner, owner, 1))

    def coded(value, rows_scale, cols_scale):
        return jnp.round(value * rows_scale * cols_scale).astype(jnp.int32).astype(jnp.int16)

    order = (2, 1, 0)
    ways = (1, 3, 1, 3)

    def chip_at(distance):
        return lax.rem(chip + distance, 4)

    def column(scale, block):
        return jnp.broadcast_to(scale[0:1, place(block)], (tile, tile)).T

    def contribution(unit, owner):
        if unit == 3:
            return owner, diagonal(owner).T
        j, part = sources(owner)[unit]
        return j, product(owner, j, part).T

    def send_far(unit):
        return remote(
            far_codes.at[unit], far_in.at[unit], far_send.at[unit], far_recv.at[unit],
            (kpt, chip_at(ways[unit]) * 2 + core),
        )

    def send_codes(joined, unit):
        distance = ways[unit] if joined else 4 - ways[unit]
        return remote(
            codes.at[joined, unit], codes_in.at[joined, unit],
            code_send.at[joined, unit], code_recv.at[joined, unit], (kpt, chip_at(distance) * 2 + core),
        )

    def coded_alone(unit, owner):
        j, value = contribution(unit, owner)
        return coded(value, scale_cols[place(owner), :], gain / scales[0:1, place(j)])

    for unit in order + (3,):
        far_codes[unit] = coded_alone(unit, chip_at(2))
        send_far(unit).start()
    for unit in order + (3,):
        codes[0, unit] = coded_alone(unit, chip_at(4 - ways[unit]))
        send_codes(0, unit).start()

    own_squares = scales[...] * scales[...]
    summed = own_squares
    for step in range(3):
        send_scales(step).wait_recv()
        summed += scales_in[step] * scales_in[step]
    sums_scale[...] = jnp.sqrt(summed)
    share_scales().start()
    for way, step in ((0, 1), (1, 2)):
        one = scales_in[step] * scales_in[step]
        passed_scale[way] = jnp.sqrt(own_squares + one)
        joined_scale[way] = jnp.sqrt(one + scales_in[0] * scales_in[0])
        ahead = chip_at(1 + 2 * way)
        turned[way] = column(scales_in.at[step], ahead) * (1.0 / LEVELS)
        turned[2 + way] = gain / column(passed_scale.at[way], ahead)

    for unit in order + (3,):
        way = ways[unit] // 2
        j, value = contribution(unit, chip_at(ways[unit]))
        send_far(unit).wait_recv()
        before = far_in[unit].astype(jnp.int32).astype(jnp.float32)
        value += before * turned[way] * scales_in[1 + way, 0:1, place(j)]
        codes[1, unit] = coded(value, turned[2 + way], gain / passed_scale[way, 0:1, place(j)])
        send_codes(1, unit).start()

    for way in range(2):
        turned[way] = column(scales_in.at[2 - way], chip) * (1.0 / LEVELS)
        turned[2 + way] = column(joined_scale.at[way], chip) * (1.0 / LEVELS)
    own_turned = column(sums_scale, chip)

    def gather(unit):
        way = ways[unit] // 2
        j, value = contribution(unit, chip)
        send_codes(0, unit).wait_recv()
        wide = codes_in[0, unit].astype(jnp.int32).astype(jnp.float32)
        value += wide * turned[way] * scales_in[2 - way, 0:1, place(j)]
        send_codes(1, unit).wait_recv()
        wide = codes_in[1, unit].astype(jnp.int32).astype(jnp.float32)
        total[unit] = value + wide * turned[2 + way] * joined_scale[way, 0:1, place(j)]

    def send_sum(unit, side):
        j = sources(chip)[unit][0]
        return remote(
            sums.at[unit, pl.ds(side * 64, 64)], sums_in.at[core, unit],
            sum_send.at[unit, side], sum_recv.at[core, unit], (kpt, j * 2 + side),
        )

    def take_sum(k, unit):
        return remote(
            sums.at[unit, pl.ds(0, 64)], sums_in.at[k, unit], sum_send.at[unit, 0], sum_recv.at[k, unit], here
        )

    for unit in order:
        j = sources(chip)[unit][0]
        gather(unit)
        sums[unit] = coded(
            (total[unit] * (gain / own_turned) * (gain / sums_scale[0:1, place(j)])).T, 1.0, 1.0
        )
        for side in range(2):
            send_sum(unit, side).start()

    def hand(unit, part, j):
        return remote(
            handed.at[unit], out.at[core, part, :, place(j)], hand_send.at[unit], hand_recv.at[unit], here
        )

    mine = pl.ds(pl.multiple_of(core * 64, 64), 64)
    theirs = pl.ds(pl.multiple_of((1 - core) * 64, 64), 64)
    final = [(unit, part, j) for unit, (j, part) in enumerate(sources(chip))]
    final += [(3, 0, chip), (4, 1, chip)]
    for unit, part, j in final[:3]:
        handed[unit] = total[unit, theirs, :] * factor
        hand(unit, part, j).start()
        out[core, part, :, place(j)] = total[unit, mine, :] * factor
    gather(3)
    packed = total[3] * factor
    turned[0] = packed.T
    strict = lax.broadcasted_iota(jnp.int32, (tile, tile), 0) > lax.broadcasted_iota(jnp.int32, (tile, tile), 1)
    real = jnp.where(strict, turned[0], packed)
    imag = jnp.where(strict, packed, 0.0)
    total[3] = real
    total[4] = imag - imag.T
    for unit, part, j in final[3:]:
        handed[unit] = total[unit, theirs, :]
        hand(unit, part, j).start()
        out[core, part, :, place(j)] = total[unit, mine, :]

    share_scales().wait_recv()
    for same in range(2):
        k = core if same == 1 else 1 - core
        scale = sums_scale if same == 1 else other_scale
        block_rows = jnp.broadcast_to(scale[0:1, place(chip)], (tile, tile)).T * (factor / LEVELS)
        turned[same] = block_rows
        down = turned[same, mine, :]
        for unit, (j, part) in enumerate(
            ((lax.rem(chip + 3, 4), 0), (lax.rem(chip + 1, 4), 1), (lax.rem(chip + 2, 4), 1 - chip // 2))
        ):
            take_sum(k, unit).wait_recv()
            wide = sums_in[k, unit].astype(jnp.int32).astype(jnp.float32)
            sign = 1 - 2 * part
            value = wide * down * scale[0:1, place(j)]
            out[k, part, :, place(j)] = value * jnp.float32(sign) if isinstance(part, int) else value * sign.astype(jnp.float32)

    share_scales().wait_send()
    for step in range(3):
        send_scales(step).wait_send()
    for unit in range(4):
        send_far(unit).wait_send()
        for joint in range(2):
            send_codes(joint, unit).wait_send()
    for unit in range(3):
        for side in range(2):
            send_sum(unit, side).wait_send()
    for unit, part, j in final:
        hand(unit, part, j).wait()
    for q in range(2):
        for t in range(MOST):
            x_piece(q, t).wait_send()
            relay(q, t).wait_send()
            if (q, t) != (1, 0):
                share(q, t).wait_send()
    whole_share().wait_send()
    for r in range(2):
        for d in (1, 2, 3):
            spread_out(r, d).wait_send()
        for p in range(naux):
            given_pair(r, p).wait_send()


def body(pairs, orbs, match):
    rounds, per_device, naux, nao, _ = pairs.shape
    nocc = orbs.shape[2] // 2
    factor = 1.0 / (rounds * naux * lax.axis_size("aux") * nocc) ** 0.5
    dma = pltpu.SemaphoreType.DMA
    combos = 2 * naux
    far_chunk = pltpu.VMEM((nao, nocc), jnp.bfloat16)
    near_chunk = pltpu.VMEM((per_device, nao, nocc), jnp.bfloat16)
    return pl.pallas_call(
        functools.partial(kernel, factor),
        out_shape=jax.ShapeDtypeStruct((per_device, 2, nao // 8, nao), jnp.float32),
        in_specs=[
            pl.BlockSpec(memory_space=pl.ANY),
            pl.BlockSpec(memory_space=pl.ANY),
            pl.BlockSpec(memory_space=pl.ANY),
        ],
        out_specs=pl.BlockSpec(memory_space=pltpu.VMEM),
        scratch_shapes=[
            pltpu.SMEM((2, 64), jnp.int32), dma,
            pltpu.VMEM((rounds, combos, nao, 2 * nao), jnp.bfloat16),
            pltpu.VMEM((per_device, nao, 2 * nocc), jnp.bfloat16),
            pltpu.VMEM((2, nao, nocc), jnp.bfloat16),
            far_chunk, far_chunk, near_chunk, near_chunk,
            pltpu.VMEM((2 * nao, nocc), jnp.bfloat16),
            pltpu.VMEM((2 * nao, rounds * combos * 2 * nocc), jnp.bfloat16),
            pltpu.VMEM((nao, 128), jnp.float32),
            pltpu.VMEM((nao, 128), jnp.float32),
            pltpu.VMEM((4, 128, 128), jnp.int16),
            pltpu.VMEM((4, 128, 128), jnp.int16),
            pltpu.VMEM((2, 4, 128, 128), jnp.int16),
            pltpu.VMEM((2, 4, 128, 128), jnp.int16),
            pltpu.VMEM((2, 8, nao), jnp.float32),
            pltpu.VMEM((2, 8, nao), jnp.float32),
            pltpu.VMEM((8, nao), jnp.float32),
            pltpu.VMEM((3, 8, nao), jnp.float32),
            pltpu.VMEM((8, nao), jnp.float32),
            pltpu.VMEM((8, nao), jnp.float32),
            pltpu.VMEM((4, 128, 128), jnp.float32),
            pltpu.VMEM((5, 128, 128), jnp.float32),
            pltpu.VMEM((3, 128, 128), jnp.int16),
            pltpu.VMEM((2, 3, 64, 128), jnp.int16),
            pltpu.VMEM((5, 64, 128), jnp.float32),
            dma((per_device,)), dma((rounds, naux)), dma((rounds, naux)), dma((rounds, naux)),
            dma((2, MOST)), dma((2, MOST)), dma((2, MOST)), dma((2, MOST)),
            dma((2, 3)), dma((2, 3)), dma((2, MOST)), dma((2, MOST)), dma((4,)), dma((4,)), dma((2, 4)), dma((2, 4)), dma((3,)), dma((3,)), dma((2,)),
            dma((3, 2)), dma((2, 3)), dma((5,)), dma((5,)),
        ],
        compiler_params=pltpu.CompilerParams(
            collective_id=0, has_side_effects=True, vmem_limit_bytes=53 << 20
        ),
    )(pairs, orbs, pltpu.with_memory_space_constraint(match, pltpu.HBM))


def solution(mesh):
    placed = (P(None, "kpt", "aux", None, None), P("kpt", None, None), P())
    return jax.shard_map(
        body, mesh=mesh, in_specs=placed, out_specs=P("kpt", None, "aux", None), check_vma=False
    )
```
